128 devices in a mesh: gx: 8 (over x, core), gy: 16 (over z, y).
Axes of the slice: x: 4, y: 4, z: 4, core: 2. Of those that a mesh axis runs over, the one named last changes fastest.
Arguments:
- state_init: float32 [4, 32, 64, 2048], P(None, None, 'gx', 'gy'), may hold values from -6 to 6
- right_side: float32 [4, 32, 64, 2048], P(None, None, 'gx', 'gy'), may hold values from -6 to 6
- rock_type: int32 [32, 64, 2048], P(None, 'gx', 'gy'), may hold values from 0 to 7
- trans_table: float32 [4, 8], replicated, may hold values from 0.25 to 4
- perf_cells: int32 [128, 128, 128], P(('gx', 'gy')), may hold values from 0 to 32767
- seg_slot: int32 [4096, 256], P(('gx', 'gy')), may hold values from 0 to 16383, as said below
- seg_inverse: float32 [4, 4, 4096, 256], P(None, None, ('gx', 'gy')), may hold values from -3 to 3
Outputs:
- state_final: float32 [4, 32, 64, 2048], P(None, None, 'gx', 'gy')
- well_rates: float32 [4, 4096, 256], P(None, ('gx', 'gy'))
The draws below stay inside these ranges and needn't reach their ends.
Inputs may be any that keep to these rules, and one draw needn't show every extreme that they name: `seg_slot`: for each owner (the wells w with the same w // 32) the positions of its segments are distinct; from each source device they name the first slots, at most 128 of them, and for every owner some source fills all 128.
All inputs are finite; a program needn't handle non-finite values.
Results may differ from the reference program's by a relative error of at most 0.0003.
Values sent between devices are 32-bit elements; how exact they have to be, the bound alone decides.
A program may use at most 128 MiB of HBM per device.

```python
import math
import jax
import jax.numpy as jnp
from jax import lax

CX = 8
CY = 128
NZ = 32
WPD = 32
SEG = 256
ROCKS = 8
NEWTON = 2
SWEEPS = 4
NX = 64
NY = 2048
WELLS = 4096
CAP = 128
CELLS_DEV = 32768
N_GY = 16
DEVICES = 128


def slot_counts(key):
    mean_load = WPD * SEG // DEVICES
    shared_key = jax.random.fold_in(key, 11)
    spread = jax.random.randint(jax.random.fold_in(shared_key, 1), (DEVICES, DEVICES // 2), 0, mean_load + 1)
    forced = jax.random.randint(jax.random.fold_in(shared_key, 2), (DEVICES,), 0, DEVICES // 2)
    forced = forced.at[0].set(DEVICES // 2 - 1)
    pair_ids = jnp.arange(DEVICES // 2, dtype=jnp.int32)[None, :]
    spread = jnp.where(pair_ids == forced[:, None], mean_load, spread)
    return jnp.stack([mean_load - spread, mean_load + spread], axis=-1).reshape(DEVICES, DEVICES).astype(jnp.int32)


def draw_seg_slot(key, part):
    counts = slot_counts(key)
    end_rows = jnp.cumsum(counts, axis=1).astype(jnp.int32)
    starts = end_rows - counts
    segment_ids = jnp.arange(WPD * SEG, dtype=jnp.int32)

    def locate(end_row, start_row):
        source = jnp.searchsorted(end_row, segment_ids, side='right').astype(jnp.int32)
        return source * CAP + segment_ids - start_row[source]
    return jax.vmap(locate)(end_rows, starts).reshape(DEVICES * WPD, SEG).astype(jnp.int32)


def set_ends(result, own_key, smallest, high):
    shape = result.shape
    spot = [jax.random.randint(jax.random.fold_in(own_key, axis), (), 0, shape[axis]) for axis in range(len(shape))]
    result = result.at[tuple(spot)].set(smallest)
    longest = shape.index(max(shape))
    spot[longest] = (spot[longest] + 1) % shape[longest]
    return result.at[tuple(spot)].set(high)


def steps_of(own_key, dims, shards, low, high):
    def one(axis_at, shards_of):
        steps = jax.random.uniform(jax.random.fold_in(jax.random.fold_in(own_key, 6), axis_at), (shards_of,), jnp.float32, low / len(shards), high / len(shards))
        return jnp.repeat(jnp.exp(steps), dims[axis_at] // shards_of).reshape((-1,) + (1,) * (len(dims) - axis_at - 1))

    loudness = one(*shards[0])
    for cut in shards[1:]:
        loudness = loudness * one(*cut)
    return loudness


def centred(rng, extent, scale, reach, cuts=(), kind=jnp.bfloat16):
    level = steps_of(rng, extent, cuts, -0.22, 0.18) if cuts else 1.0
    array = jax.random.normal(rng, extent, jnp.float32) * scale * level
    return jnp.minimum(jnp.maximum(array, -reach), reach).astype(kind)


def setup_inputs(seed: int = 0) -> dict:
    arg_keys = jax.random.split(jax.random.key(seed), 8)
    return {
        "state_init": centred(arg_keys[0], (4, NZ, NX, NY), 1.0, 6.0, ((2, 8), (3, 16)), jnp.float32),
        "right_side": centred(arg_keys[1], (4, NZ, NX, NY), 1.0, 6.0, ((2, 8), (3, 16)), jnp.float32),
        "rock_type": set_ends(jax.random.randint(arg_keys[2], (NZ, NX, NY), 0, ROCKS), jax.random.fold_in(arg_keys[2], 1), 0, ROCKS - 1).astype(jnp.int32),
        "trans_table": jnp.clip(jnp.exp(jax.random.uniform(arg_keys[3], (4, ROCKS), jnp.float32, math.log(0.25), math.log(4.0))), 0.25, 4.0),
        "perf_cells": set_ends(jax.random.randint(arg_keys[4], (DEVICES, DEVICES, CAP), 0, CELLS_DEV), jax.random.fold_in(arg_keys[4], 1), 0, CELLS_DEV - 1).astype(jnp.int32),
        "seg_slot": draw_seg_slot(jax.random.fold_in(arg_keys[7], 71), 0),
        "seg_inverse": centred(arg_keys[6], (4, 4, WELLS, SEG), 0.5, 3.0, ((2, 128),), jnp.float32),
    }


def coefficient(rock_type, trans_table):
    total = jnp.zeros((trans_table.shape[0],) + rock_type.shape, jnp.float32)
    for rock_kind in range(trans_table.shape[1]):
        picked = jnp.where(rock_type == rock_kind, 1.0, 0.0).astype(jnp.float32)
        total = total + picked[None] * trans_table[:, rock_kind][:, None, None, None]
    return 6.0 + total


def decay_matrix(count):
    first = jnp.arange(count, dtype=jnp.int32)[:, None]
    second = jnp.arange(count, dtype=jnp.int32)[None, :]
    gap = (second - first).astype(jnp.float32)
    return jnp.where(gap >= 0, 0.3 * jnp.power(jnp.float32(0.9), jnp.maximum(gap, 0.0)), 0.0).astype(jnp.float32)


def neighbour_sum(padded):
    total = padded[:, 2:, 1:-1, 1:-1] + padded[:, :-2, 1:-1, 1:-1]
    total = total + padded[:, 1:-1, 2:, 1:-1] + padded[:, 1:-1, :-2, 1:-1]
    return total + padded[:, 1:-1, 1:-1, 2:] + padded[:, 1:-1, 1:-1, :-2]


def padded_all(values):
    return jnp.pad(values, ((0, 0), (1, 1), (1, 1), (1, 1)))


def segment_rates(rows, seg_inverse, decay):
    flow = jnp.sum(seg_inverse * rows[None], axis=1)
    shaped = flow.reshape(-1, flow.shape[2])
    return jnp.dot(shaped, decay, precision=lax.Precision.HIGHEST).reshape(flow.shape)


def reference(state_init, right_side, rock_type, trans_table, perf_cells, seg_slot, seg_inverse):
    coeff = coefficient(rock_type, trans_table)
    decay = decay_matrix(SEG)
    owner_ids = (jnp.arange(WELLS, dtype=jnp.int32) // WPD)[:, None]
    source_dev = (seg_slot // CAP).astype(jnp.int32)
    slot_ids = (seg_slot % CAP).astype(jnp.int32)
    local_cell = perf_cells[source_dev, owner_ids, slot_ids]
    seg_z = local_cell // (CX * CY)
    seg_x = (source_dev // N_GY) * CX + (local_cell // CY) % CX
    seg_y = (source_dev % N_GY) * CY + local_cell % CY
    state = state_init
    rates = jnp.zeros((4, WELLS, SEG), jnp.float32)
    for newton_step in range(NEWTON):
        rows = state[:, seg_z, seg_x, seg_y]
        rates = segment_rates(rows, seg_inverse, decay)
        inflow = jnp.zeros_like(state).at[:, seg_z, seg_x, seg_y].add(rates)
        forcing = coeff * state - neighbour_sum(padded_all(state)) + 0.1 * state * state * state - right_side - inflow
        jacobi = coeff + 0.3 * state * state
        correction = forcing / jacobi
        for sweep_step in range(SWEEPS - 1):
            correction = (forcing + neighbour_sum(padded_all(correction))) / jacobi
        state = state - correction
    return state, rates
```

```python
import functools

import jax
import jax.numpy as jnp
from jax import lax
from jax.experimental import pallas as pl
from jax.experimental.pallas import tpu as pltpu
from jax.sharding import PartitionSpec as P

NEWTON = 2
SWEEPS = 4
GROUPS = 4
STEP = 8
F32 = jnp.float32
BF16 = jnp.bfloat16
MESH = pl.DeviceIdType.MESH


def halves(x):
    high = x.astype(BF16)
    return high, (x - high.astype(F32)).astype(BF16)


def onehot(size, index):
    rows = lax.broadcasted_iota(jnp.int32, (size, index.shape[1]), 0)
    return jnp.where(rows == index, 1.0, 0.0).astype(BF16)


def kernel(
    n_gx, n_gy, layers, wells,
    state_in, right, rock, table, cells, slots, inverse,
    state_out, rates_out,
    coeff, forcing, factor, corr, split, send1, recv1, split2, rows, send2, recv2, total3, total4, decay,
    xs, xr, ys, yr,
    send1_sem, recv1_sem, send2_sem, recv2_sem, rim_send, rim_recv,
):
    gx, gy = lax.axis_index("gx"), lax.axis_index("gy")
    devices = n_gx * n_gy
    me = gx * n_gy + gy
    cell_rows = layers * 8
    tiles = 4 * layers
    group = devices // GROUPS
    my_group = lax.div(me, group)

    def place(device):
        return (lax.div(device, n_gy), lax.rem(device, n_gy))

    barrier = pltpu.get_barrier_semaphore()

    def greet(step, carry):
        pl.semaphore_signal(
            barrier, inc=1, device_id=place(lax.rem(me + step, devices)), device_id_type=MESH
        )
        return carry

    lax.fori_loop(1, devices, greet, 0)

    for c in range(4):
        value = jnp.full((cell_rows, 128), 6.0, F32)
        for kind in range(8):
            value = value + jnp.where(rock[...] == kind, table[c, kind], 0.0)
        coeff[c * cell_rows : (c + 1) * cell_rows, :] = value
    state_out[...] = state_in[...]
    first = lax.broadcasted_iota(jnp.int32, decay.shape, 0)
    second = lax.broadcasted_iota(jnp.int32, decay.shape, 1)
    gap = (second - first).astype(F32)
    decay[...] = jnp.where(
        gap >= 0, 0.3 * jnp.exp(jnp.maximum(gap, 0.0) * -0.10536051565782628), 0.0
    )
    pl.semaphore_wait(barrier, devices - 1)

    lane = lax.broadcasted_iota(jnp.int32, (8, 128), 1)
    sub = lax.broadcasted_iota(jnp.int32, (8, 128), 0)

    def rim_copies(turn):
        right_x = (lax.rem(gx + 1, n_gx), gy)
        left_x = (lax.rem(gx + n_gx - 1, n_gx), gy)
        right_y = (gx, lax.rem(gy + 1, n_gy))
        left_y = (gx, lax.rem(gy + n_gy - 1, n_gy))
        plan = ((xs, xr, 1, 0, right_x), (xs, xr, 0, 1, left_x), (ys, yr, 1, 0, right_y), (ys, yr, 0, 1, left_y))
        return [
            pltpu.make_async_remote_copy(
                src_ref=src.at[turn, out_side],
                dst_ref=dst.at[turn, in_side],
                send_sem=rim_send.at[turn, k],
                recv_sem=rim_recv.at[turn, k],
                device_id=target,
                device_id_type=MESH,
            )
            for k, (src, dst, out_side, in_side, target) in enumerate(plan)
        ]

    def pack_lanes(i, value, packed):
        low, high = packed
        low = jnp.where(lane == i, pltpu.roll(value, i, axis=1), low)
        high = jnp.where(lane == i, pltpu.roll(value, lax.rem(i + 1, 128), axis=1), high)
        return low, high

    def send_rims(turn, field, packed):
        xs[turn, 0] = field[pl.ds(0, tiles, stride=8), :]
        xs[turn, 1] = field[pl.ds(7, tiles, stride=8), :]
        ys[turn, 0] = packed[0]
        ys[turn, 1] = packed[1]
        for copy in rim_copies(turn):
            copy.start()

    def wait_rims(turn):
        for copy in rim_copies(turn):
            copy.wait()

    def mask_rims(turn):
        for side, edge_x, edge_y in ((0, 0, 0), (1, n_gx - 1, n_gy - 1)):
            xr[turn, side] = jnp.where(gx == edge_x, 0.0, xr[turn, side])
            yr[turn, side] = jnp.where(gy == edge_y, 0.0, yr[turn, side])

    zero_packed = (jnp.zeros((8, 128), F32), jnp.zeros((8, 128), F32))

    def tile_at(field, i):
        return field[pl.ds(pl.multiple_of(i * 8, 8), 8), :]

    def neighbours(turn, field, i):
        value = tile_at(field, i)
        layer = lax.rem(i, layers)
        above = tile_at(field, jnp.maximum(i - 1, 0))
        below = tile_at(field, jnp.minimum(i + 1, tiles - 1))
        total = jnp.where(layer > 0, above, 0.0) + jnp.where(layer < layers - 1, below, 0.0)
        x_low = jnp.broadcast_to(xr[turn, 0, pl.ds(i, 1), :], (8, 128))
        x_high = jnp.broadcast_to(xr[turn, 1, pl.ds(i, 1), :], (8, 128))
        total = total + jnp.where(sub == 0, x_low, pltpu.roll(value, 1, axis=0))
        total = total + jnp.where(sub == 7, x_high, pltpu.roll(value, 7, axis=0))
        y_low = pltpu.roll(yr[turn, 0], lax.rem(128 - i, 128), axis=1)
        y_high = pltpu.roll(yr[turn, 1], 127 - i, axis=1)
        total = total + jnp.where(lane == 0, y_low, pltpu.roll(value, 1, axis=1))
        return value, total + jnp.where(lane == 127, y_high, pltpu.roll(value, 127, axis=1))

    def block_copy(source, target, source_slot, target_slot, device, send_sem, recv_sem):
        return pltpu.make_async_remote_copy(
            src_ref=source.at[source_slot],
            dst_ref=target.at[target_slot],
            send_sem=send_sem,
            recv_sem=recv_sem,
            device_id=place(device),
            device_id_type=MESH,
        )

    def newton(n, carry):
        turn = n * SWEEPS

        def pack_state(i, packed):
            return pack_lanes(i, tile_at(state_out, i), packed)

        send_rims(turn, state_out, lax.fori_loop(0, tiles, pack_state, zero_packed, unroll=4))

        for c in range(4):
            high, low = halves(state_out[c * cell_rows : (c + 1) * cell_rows, :])
            split[c, :, 0:128] = high
            split[c, :, 128:256] = low

        def gather_pair(pair):
            index = jnp.concatenate([cells[pl.ds(2 * pair + k, 1), :] for k in range(2)], axis=1)
            pick = onehot(128, index & 127)
            pick = jnp.concatenate([pick, pick], axis=0)
            wanted = lax.broadcasted_iota(jnp.int32, (cell_rows, 256), 0) == (index >> 7)
            found = []
            for c in range(4):
                value = jnp.dot(split[c], pick, preferred_element_type=F32)
                found.append(jnp.sum(jnp.where(wanted, value, 0.0), axis=0, keepdims=True))
            found = jnp.concatenate(found, axis=0)
            return found[:, :128], found[:, 128:]

        my_pair = lax.div(me, 2)
        pairs = devices // 2

        def gather_step(step, inner):
            pair = lax.rem(my_pair + 1 + step, pairs)
            for k, block in enumerate(gather_pair(pair)):
                send1[n, 2 * pair + k] = block
                block_copy(
                    send1.at[n], recv1.at[n], 2 * pair + k, me, 2 * pair + k, send1_sem.at[n], recv1_sem.at[n]
                ).start()
            return inner

        lax.fori_loop(0, pairs - 1, gather_step, 0)
        for k, block in enumerate(gather_pair(my_pair)):
            send1[n, 2 * my_pair + k] = block
        partner = 4 * my_pair + 1 - me
        block_copy(
            send1.at[n], recv1.at[n], partner, me, partner, send1_sem.at[n], recv1_sem.at[n]
        ).start()
        recv1[n, me] = send1[n, me]

        wait_rims(turn)
        mask_rims(turn)

        def base(i, inner):
            value, near = neighbours(turn, state_out, i)
            at = pl.ds(pl.multiple_of(i * 8, 8), 8)
            square = value * value
            forcing[at, :] = coeff[at, :] * value - near + 0.1 * square * value - right[at, :]
            factor[at, :] = 1.0 / (coeff[at, :] + 0.3 * square)
            return inner

        lax.fori_loop(0, tiles, base, 0, unroll=4)

        all_blocks = pl.ds(0, devices - 1)
        arrived = pltpu.make_async_remote_copy(
            src_ref=send1.at[n, all_blocks],
            dst_ref=recv1.at[n, all_blocks],
            send_sem=send1_sem.at[n],
            recv_sem=recv1_sem.at[n],
            device_id=place(me),
            device_id_type=MESH,
        )
        arrived.wait_recv()

        high, low = halves(recv1[n].reshape(4 * devices, 128))
        split2[:, 0:128] = high
        split2[:, 128:256] = low
        quarter = lax.broadcasted_iota(jnp.int32, (4 * devices, 256), 0) >> 2

        def owner_gather(w, inner):
            index = slots[pl.ds(w, 1), :]
            pick = onehot(128, index & 127)
            pick = jnp.concatenate([pick, pick], axis=0)
            value = jnp.dot(split2[...], pick, preferred_element_type=F32)
            value = jnp.where(quarter == (index >> 7), value, 0.0)
            value = jnp.sum(value.reshape(devices // 2, 8, 256), axis=0)
            value = value[0:4] + value[4:8]
            rows[0, pl.ds(w, 4, stride=wells), :] = value[:, :128]
            rows[1, pl.ds(w, 4, stride=wells), :] = value[:, 128:]
            return inner

        lax.fori_loop(0, wells, owner_gather, 0)
        flows = []
        for i in range(4):
            sides = []
            for half in range(2):
                at = slice(half * 128, half * 128 + 128)
                flow = inverse[i, 0, :, at] * rows[half, 0:wells, :]
                for j in range(1, 4):
                    flow = flow + inverse[i, j, :, at] * rows[half, j * wells : (j + 1) * wells, :]
                sides.append(flow)
            flows.append(jnp.concatenate(sides, axis=1))
        rates = jnp.dot(
            jnp.concatenate(flows, axis=0),
            decay[...],
            precision=lax.Precision.HIGHEST,
            preferred_element_type=F32,
        )
        rates_out[...] = rates
        rows[0] = rates[:, :128]
        rows[1] = rates[:, 128:]
        total3[...] = jnp.zeros_like(total3)

        def owner_scatter(w, inner):
            index = slots[pl.ds(w, 1), :]
            pick = onehot(128, index & 127)
            rate = jnp.concatenate([rows[k, pl.ds(w, 4, stride=wells), :] for k in range(2)], axis=1)
            rate = jnp.concatenate([rate, rate], axis=0)
            wanted = quarter == (index >> 7)
            parts = []
            for half in halves(rate):
                spread = jnp.broadcast_to(half.astype(F32)[None], (devices // 2, 8, 256))
                spread = spread.reshape(4 * devices, 256)
                parts.append(jnp.where(wanted, spread, 0.0).astype(BF16))
            total3[...] += lax.dot_general(
                jnp.concatenate(parts, axis=1),
                jnp.concatenate([pick, pick], axis=1),
                (((1,), (1,)), ((), ())),
                preferred_element_type=F32,
            )
            return inner

        lax.fori_loop(0, wells, owner_scatter, 0)
        send2[n] = total3[...].reshape(devices, 4, 128)
        recv2[n, me] = send2[n, me]

        def return_step(step, inner):
            j = lax.div(step, group)
            target = lax.rem(my_group + j, GROUPS) * group + lax.rem(me + step, group)
            block_copy(
                send2.at[n], recv2.at[n], target, me, target, send2_sem.at[n], recv2_sem.at[n, j]
            ).start()
            return inner

        lax.fori_loop(1, devices, return_step, 0)
        arrived.wait_send()

        total4[...] = jnp.zeros_like(total4)

        def wait_group(j, count):
            some = pl.ds(0, count)
            pltpu.make_async_remote_copy(
                src_ref=send2.at[n, some],
                dst_ref=recv2.at[n, some],
                send_sem=send2_sem.at[n],
                recv_sem=recv2_sem.at[n, j],
                device_id=place(me),
                device_id_type=MESH,
            ).wait_recv()

        def inflow_group(j):
            start = lax.rem(my_group + GROUPS - j, GROUPS) * group

            def inflow_step(step, inner):
                owner = start + step * STEP
                index = jnp.concatenate([cells[pl.ds(owner + k, 1), :] for k in range(STEP)], axis=1)
                value = jnp.concatenate([recv2[n, owner + k] for k in range(STEP)], axis=1)
                lanes = onehot(128, index & 127)
                pick = onehot(cell_rows, index >> 7)
                pick = jnp.concatenate([pick, pick], axis=1)
                high, low = halves(value)
                for c in range(4):
                    spread = jnp.concatenate([lanes * high[c : c + 1], lanes * low[c : c + 1]], axis=1)
                    total4[c] += lax.dot_general(
                        spread, pick, (((1,), (1,)), ((), ())), preferred_element_type=F32
                    )
                return inner

            lax.fori_loop(0, group // STEP, inflow_step, 0)

        wait_group(0, group - 1)
        inflow_group(0)
        for j in range(1, GROUPS):
            wait_group(j, group)
            inflow_group(j)
        sent = pl.ds(0, devices - 1)
        pltpu.make_async_remote_copy(
            src_ref=send2.at[n, sent],
            dst_ref=recv2.at[n, sent],
            send_sem=send2_sem.at[n],
            recv_sem=recv2_sem.at[n, 0],
            device_id=place(me),
            device_id_type=MESH,
        ).wait_send()

        for c in range(4):
            at = slice(c * cell_rows, (c + 1) * cell_rows)
            forcing[at, :] = forcing[at, :] - total4[c].T

        def first_sweep(i, packed):
            at = pl.ds(pl.multiple_of(i * 8, 8), 8)
            value = forcing[at, :] * factor[at, :]
            corr[0, at, :] = value
            return pack_lanes(i, value, packed)

        packed = lax.fori_loop(0, tiles, first_sweep, zero_packed, unroll=4)
        for k in range(1, SWEEPS):
            now, later = corr.at[(k - 1) % 2], corr.at[k % 2]
            send_rims(turn + k, now, packed)
            wait_rims(turn + k)
            mask_rims(turn + k)

            def sweep(i, packed):
                at = pl.ds(pl.multiple_of(i * 8, 8), 8)
                _, near = neighbours(turn + k, now, i)
                value = (forcing[at, :] + near) * factor[at, :]
                if k == SWEEPS - 1:
                    state_out[at, :] = state_out[at, :] - value
                    return packed
                later[at, :] = value
                return pack_lanes(i, value, packed)

            packed = lax.fori_loop(0, tiles, sweep, zero_packed, unroll=4)
        return carry

    lax.fori_loop(0, NEWTON, newton, 0)


def on_device(n_gx, n_gy, state_init, right_side, rock_type, trans_table, perf_cells, seg_slot, seg_inverse):
    channels, layers, rows, columns = state_init.shape
    devices = n_gx * n_gy
    wells, segments = seg_slot.shape
    cell_rows = layers * rows
    tiles = channels * layers
    field = (channels * cell_rows, columns)
    vmem = pl.BlockSpec(memory_space=pltpu.VMEM)
    smem = pl.BlockSpec(memory_space=pltpu.SMEM)
    turns = NEWTON * SWEEPS
    dma = pltpu.SemaphoreType.DMA
    state, rates = pl.pallas_call(
        functools.partial(kernel, n_gx, n_gy, layers, wells),
        out_shape=(
            jax.ShapeDtypeStruct(field, F32),
            jax.ShapeDtypeStruct((channels * wells, segments), F32),
        ),
        in_specs=[vmem, vmem, vmem, smem, vmem, vmem, vmem],
        out_specs=(vmem, vmem),
        scratch_shapes=[
            pltpu.VMEM(field, F32),
            pltpu.VMEM(field, F32),
            pltpu.VMEM(field, F32),
            pltpu.VMEM((2,) + field, F32),
            pltpu.VMEM((channels, cell_rows, 256), BF16),
            pltpu.VMEM((NEWTON, devices, channels, 128), F32),
            pltpu.VMEM((NEWTON, devices, channels, 128), F32),
            pltpu.VMEM((channels * devices, 256), BF16),
            pltpu.VMEM((2, channels * wells, 128), F32),
            pltpu.VMEM((NEWTON, devices, channels, 128), F32),
            pltpu.VMEM((NEWTON, devices, channels, 128), F32),
            pltpu.VMEM((channels * devices, 128), F32),
            pltpu.VMEM((channels, 128, cell_rows), F32),
            pltpu.VMEM((segments, segments), F32),
            pltpu.VMEM((turns, 2, tiles, 128), F32),
            pltpu.VMEM((turns, 2, tiles, 128), F32),
            pltpu.VMEM((turns, 2, 8, 128), F32),
            pltpu.VMEM((turns, 2, 8, 128), F32),
            dma((NEWTON,)),
            dma((NEWTON,)),
            dma((NEWTON,)),
            dma((NEWTON, GROUPS)),
            dma((turns, 4)),
            dma((turns, 4)),
        ],
        compiler_params=pltpu.CompilerParams(
            collective_id=0, has_side_effects=True, vmem_limit_bytes=48 * 1024 * 1024
        ),
        name="newton",
    )(
        state_init.reshape(field),
        right_side.reshape(field),
        rock_type.reshape(cell_rows, columns),
        trans_table,
        perf_cells.reshape(devices, perf_cells.shape[2]),
        seg_slot,
        seg_inverse,
    )
    return state.reshape(state_init.shape), rates.reshape(channels, wells, segments)


def solution(mesh):
    in_specs = (
        P(None, None, "gx", "gy"),
        P(None, None, "gx", "gy"),
        P(None, "gx", "gy"),
        P(),
        P(("gx", "gy"), None, None),
        P(("gx", "gy"), None),
        P(None, None, ("gx", "gy"), None),
    )
    out_specs = (P(None, None, "gx", "gy"), P(None, ("gx", "gy"), None))
    return jax.shard_map(
        functools.partial(on_device, mesh.shape["gx"], mesh.shape["gy"]),
        mesh=mesh,
        in_specs=in_specs,
        out_specs=out_specs,
        check_vma=False,
    )
```

```python
import functools

import jax
import jax.numpy as jnp
from jax import lax
from jax.experimental import pallas as pl
from jax.experimental.pallas import tpu as pltpu
from jax.sharding import PartitionSpec as P

NEWTON = 2
SWEEPS = 4
GROUPS = 4
STEP = 16
WELLS_STEP = 8
F32 = jnp.float32
BF16 = jnp.bfloat16
MESH = pl.DeviceIdType.MESH


def halves(x):
    high = x.astype(BF16)
    return high, (x - high.astype(F32)).astype(BF16)


def onehot(size, index):
    rows = lax.broadcasted_iota(jnp.int32, (size, index.shape[1]), 0)
    return jnp.where(rows == index, 1.0, 0.0).astype(BF16)


def kernel(
    n_gx, n_gy, layers, wells,
    state_in, right_in, rock_in, table, cells_in, slots_in, inverse_in,
    state_out, rates_out,
    right, rock, cells, slots, inverse, load_sem,
    coeff, forcing, factor, corr, split, send1, recv1, split2, rows, send2, recv2, total3, total4, decay,
    xs, xr, ys, yr,
    send1_sem, recv1_sem, send2_sem, recv2_sem, rim_send, rim_recv,
):
    gx, gy = lax.axis_index("gx"), lax.axis_index("gy")
    devices = n_gx * n_gy
    me = gx * n_gy + gy
    cell_rows = layers * 8
    tiles = 4 * layers
    group = devices // GROUPS
    my_group = lax.div(me, group)

    def place(device):
        return (lax.div(device, n_gy), lax.rem(device, n_gy))

    loads = [
        pltpu.make_async_copy(source, target, load_sem.at[k])
        for k, (source, target) in enumerate(
            (
                (rock_in, rock),
                (state_in, state_out),
                (cells_in, cells),
                (right_in, right),
                (slots_in, slots),
                (inverse_in, inverse),
            )
        )
    ]
    for load in loads:
        load.start()

    barrier = pltpu.get_barrier_semaphore()

    def greet(step, carry):
        pl.semaphore_signal(
            barrier, inc=1, device_id=place(lax.rem(me + step, devices)), device_id_type=MESH
        )
        return carry

    lax.fori_loop(1, devices, greet, 0)

    loads[0].wait()

    def coefficients(i, inner):
        at = pl.ds(pl.multiple_of(i * 8, 8), 8)
        kinds = rock[at, :]
        picked = [kinds == kind for kind in range(8)]
        for c in range(4):
            value = jnp.full((8, 128), 6.0, F32)
            for kind in range(8):
                value = value + jnp.where(picked[kind], table[c, kind], 0.0)
            coeff[pl.ds(pl.multiple_of(c * cell_rows + i * 8, 8), 8), :] = value
        return inner

    lax.fori_loop(0, layers, coefficients, 0, unroll=2)
    first = lax.broadcasted_iota(jnp.int32, decay.shape, 0)
    second = lax.broadcasted_iota(jnp.int32, decay.shape, 1)
    gap = (second - first).astype(F32)
    decay[...] = jnp.where(
        gap >= 0, 0.3 * jnp.exp(jnp.maximum(gap, 0.0) * -0.10536051565782628), 0.0
    )
    for load in loads[1:]:
        load.wait()
    pl.semaphore_wait(barrier, devices - 1)

    lane = lax.broadcasted_iota(jnp.int32, (8, 128), 1)
    sub = lax.broadcasted_iota(jnp.int32, (8, 128), 0)

    def rim_copies(turn):
        right_x = (lax.rem(gx + 1, n_gx), gy)
        left_x = (lax.rem(gx + n_gx - 1, n_gx), gy)
        right_y = (gx, lax.rem(gy + 1, n_gy))
        left_y = (gx, lax.rem(gy + n_gy - 1, n_gy))
        plan = ((xs, xr, 1, 0, right_x), (xs, xr, 0, 1, left_x), (ys, yr, 1, 0, right_y), (ys, yr, 0, 1, left_y))
        return [
            pltpu.make_async_remote_copy(
                src_ref=src.at[turn, out_side],
                dst_ref=dst.at[turn, in_side],
                send_sem=rim_send.at[turn, k],
                recv_sem=rim_recv.at[turn, k],
                device_id=target,
                device_id_type=MESH,
            )
            for k, (src, dst, out_side, in_side, target) in enumerate(plan)
        ]

    def for_tiles(body):
        def channel(c, packed):
            low, high = jnp.zeros((8, 128), F32), jnp.zeros((8, 128), F32)
            edge = None
            for z in range(layers):
                at = pl.ds(pl.multiple_of(c * cell_rows + z * 8, 8), 8)
                edge = body(c, z, at)
                if edge is not None:
                    low = jnp.where(lane == z, pltpu.roll(edge, z, axis=1) if z else edge, low)
                    high = jnp.where(lane == z, pltpu.roll(edge, z + 1, axis=1), high)
            if edge is None:
                return packed
            ours = (lane >= c * layers) & (lane < (c + 1) * layers)
            low = jnp.where(ours, pltpu.roll(low, c * layers, axis=1), packed[0])
            high = jnp.where(ours, pltpu.roll(high, c * layers, axis=1), packed[1])
            return low, high

        return lax.fori_loop(0, 4, channel, zero_packed)

    def send_rims(turn, field, packed):
        xs[turn, 0] = field[pl.ds(0, tiles, stride=8), :]
        xs[turn, 1] = field[pl.ds(7, tiles, stride=8), :]
        ys[turn, 0] = packed[0]
        ys[turn, 1] = packed[1]
        for copy in rim_copies(turn):
            copy.start()

    def wait_rims(turn):
        for copy in rim_copies(turn):
            copy.wait()

    def mask_rims(turn):
        for side, edge_x, edge_y in ((0, 0, 0), (1, n_gx - 1, n_gy - 1)):
            xr[turn, side] = jnp.where(gx == edge_x, 0.0, xr[turn, side])
            yr[turn, side] = jnp.where(gy == edge_y, 0.0, yr[turn, side])

    zero_packed = (jnp.zeros((8, 128), F32), jnp.zeros((8, 128), F32))

    def neighbours(turn, field, c, z, at):
        value = field[at, :]
        row = c * layers + z
        y_low = pltpu.roll(yr[turn, 0], lax.rem(128 - row, 128), axis=1)
        y_high = pltpu.roll(yr[turn, 1], 127 - row, axis=1)
        total = jnp.where(sub == 0, jnp.broadcast_to(xr[turn, 0, pl.ds(row, 1), :], (8, 128)), pltpu.roll(value, 1, axis=0))
        total = total + jnp.where(
            sub == 7, jnp.broadcast_to(xr[turn, 1, pl.ds(row, 1), :], (8, 128)), pltpu.roll(value, 7, axis=0)
        )
        total = total + jnp.where(lane == 0, y_low, pltpu.roll(value, 1, axis=1))
        total = total + jnp.where(lane == 127, y_high, pltpu.roll(value, 127, axis=1))
        if z > 0:
            total = total + field[pl.ds(pl.multiple_of(c * cell_rows + z * 8 - 8, 8), 8), :]
        if z < layers - 1:
            total = total + field[pl.ds(pl.multiple_of(c * cell_rows + z * 8 + 8, 8), 8), :]
        return value, total

    def block_copy(source, target, source_slot, target_slot, device, send_sem, recv_sem):
        return pltpu.make_async_remote_copy(
            src_ref=source.at[source_slot],
            dst_ref=target.at[target_slot],
            send_sem=send_sem,
            recv_sem=recv_sem,
            device_id=place(device),
            device_id_type=MESH,
        )

    def newton(n, carry):
        turn = n * SWEEPS

        send_rims(turn, state_out, for_tiles(lambda c, z, at: state_out[at, :]))

        for c in range(4):
            high, low = halves(state_out[c * cell_rows : (c + 1) * cell_rows, :])
            split[c, :, 0:128] = high
            split[c, :, 128:256] = low

        def gather_pair(pair):
            index = jnp.concatenate([cells[pl.ds(2 * pair + k, 1), :] for k in range(2)], axis=1)
            pick = onehot(128, index & 127)
            pick = jnp.concatenate([pick, pick], axis=0)
            wanted = lax.broadcasted_iota(jnp.int32, (cell_rows, 256), 0) == (index >> 7)
            found = []
            for c in range(4):
                value = jnp.dot(split[c], pick, preferred_element_type=F32)
                found.append(jnp.sum(jnp.where(wanted, value, 0.0), axis=0, keepdims=True))
            found = jnp.concatenate(found, axis=0)
            return found[:, :128], found[:, 128:]

        my_pair = lax.div(me, 2)
        pairs = devices // 2

        def gather_step(step, inner):
            pair = lax.rem(my_pair + 1 + step, pairs)
            for k, block in enumerate(gather_pair(pair)):
                send1[n, 2 * pair + k] = block
                block_copy(
                    send1.at[n], recv1.at[n], 2 * pair + k, me, 2 * pair + k, send1_sem.at[n], recv1_sem.at[n]
                ).start()
            return inner

        lax.fori_loop(0, pairs - 1, gather_step, 0, unroll=7)
        for k, block in enumerate(gather_pair(my_pair)):
            send1[n, 2 * my_pair + k] = block
        partner = 4 * my_pair + 1 - me
        block_copy(
            send1.at[n], recv1.at[n], partner, me, partner, send1_sem.at[n], recv1_sem.at[n]
        ).start()
        recv1[n, me] = send1[n, me]

        wait_rims(turn)
        mask_rims(turn)

        def base(c, z, at):
            value, near = neighbours(turn, state_out, c, z, at)
            square = value * value
            forcing[at, :] = coeff[at, :] * value - near + 0.1 * square * value - right[at, :]
            factor[at, :] = 1.0 / (coeff[at, :] + 0.3 * square)

        for_tiles(base)

        all_blocks = pl.ds(0, devices - 1)
        arrived = pltpu.make_async_remote_copy(
            src_ref=send1.at[n, all_blocks],
            dst_ref=recv1.at[n, all_blocks],
            send_sem=send1_sem.at[n],
            recv_sem=recv1_sem.at[n],
            device_id=place(me),
            device_id_type=MESH,
        )
        arrived.wait_recv()

        high, low = halves(recv1[n].reshape(4 * devices, 128))
        split2[:, 0:128] = high
        split2[:, 128:256] = low
        quarter = lax.broadcasted_iota(jnp.int32, (4 * devices, 256), 0) >> 2

        def owner_gather(w, inner):
            index = slots[pl.ds(w, 1), :]
            pick = onehot(128, index & 127)
            pick = jnp.concatenate([pick, pick], axis=0)
            value = jnp.dot(split2[...], pick, preferred_element_type=F32)
            value = jnp.where(quarter == (index >> 7), value, 0.0)
            value = jnp.sum(value.reshape(devices // 2, 8, 256), axis=0)
            value = value[0:4] + value[4:8]
            rows[0, pl.ds(w, 4, stride=wells), :] = value[:, :128]
            rows[1, pl.ds(w, 4, stride=wells), :] = value[:, 128:]
            return inner

        lax.fori_loop(0, wells, owner_gather, 0, unroll=4)
        flows = []
        for i in range(4):
            sides = []
            for half in range(2):
                at = slice(half * 128, half * 128 + 128)
                flow = inverse[i, 0, :, at] * rows[half, 0:wells, :]
                for j in range(1, 4):
                    flow = flow + inverse[i, j, :, at] * rows[half, j * wells : (j + 1) * wells, :]
                sides.append(flow)
            flows.append(jnp.concatenate(sides, axis=1))
        rates = jnp.dot(
            jnp.concatenate(flows, axis=0),
            decay[...],
            precision=lax.Precision.HIGHEST,
            preferred_element_type=F32,
        )
        rates_out[...] = rates
        rows[0] = rates[:, :128]
        rows[1] = rates[:, 128:]
        total3[...] = jnp.zeros_like(total3)

        def owner_scatter(step, inner):
            first_well = step * WELLS_STEP
            width = WELLS_STEP * 256
            index = jnp.concatenate([slots[pl.ds(first_well + k, 1), :] for k in range(WELLS_STEP)], axis=1)
            rate = jnp.concatenate(
                [rows[half, pl.ds(first_well + k, 4, stride=wells), :] for k in range(WELLS_STEP) for half in range(2)],
                axis=1,
            )
            pick = onehot(128, index & 127)
            wanted = (lax.broadcasted_iota(jnp.int32, (4 * devices, width), 0) >> 2) == (index >> 7)
            parts = []
            for half in halves(jnp.concatenate([rate, rate], axis=0)):
                spread = jnp.broadcast_to(half.astype(F32)[None], (devices // 2, 8, width))
                parts.append(jnp.where(wanted, spread.reshape(4 * devices, width), 0.0).astype(BF16))
            total3[...] += lax.dot_general(
                jnp.concatenate(parts, axis=1),
                jnp.concatenate([pick, pick], axis=1),
                (((1,), (1,)), ((), ())),
                preferred_element_type=F32,
            )
            return inner

        lax.fori_loop(0, wells // WELLS_STEP, owner_scatter, 0)
        send2[n] = total3[...].reshape(devices, 4, 128)
        recv2[n, me] = send2[n, me]

        def return_step(step, inner):
            j = lax.div(step, group)
            target = lax.rem(my_group + j, GROUPS) * group + lax.rem(me + step, group)
            block_copy(
                send2.at[n], recv2.at[n], target, me, target, send2_sem.at[n], recv2_sem.at[n, j]
            ).start()
            return inner

        lax.fori_loop(1, devices, return_step, 0)
        arrived.wait_send()

        total4[...] = jnp.zeros_like(total4)

        def wait_group(j, count):
            some = pl.ds(0, count)
            pltpu.make_async_remote_copy(
                src_ref=send2.at[n, some],
                dst_ref=recv2.at[n, some],
                send_sem=send2_sem.at[n],
                recv_sem=recv2_sem.at[n, j],
                device_id=place(me),
                device_id_type=MESH,
            ).wait_recv()

        def inflow_group(j):
            start = lax.rem(my_group + GROUPS - j, GROUPS) * group

            def inflow_step(step, inner):
                owner = start + step * STEP
                index = jnp.concatenate([cells[pl.ds(owner + k, 1), :] for k in range(STEP)], axis=1)
                value = jnp.concatenate([recv2[n, owner + k] for k in range(STEP)], axis=1)
                lanes = onehot(128, index & 127)
                pick = onehot(cell_rows, index >> 7)
                pick = jnp.concatenate([pick, pick], axis=1)
                high, low = halves(value)
                spread = jnp.concatenate(
                    [
                        jnp.concatenate([lanes * high[c : c + 1], lanes * low[c : c + 1]], axis=1)
                        for c in range(4)
                    ],
                    axis=0,
                )
                total4[...] += lax.dot_general(
                    pick, spread, (((1,), (1,)), ((), ())), preferred_element_type=F32
                )
                return inner

            lax.fori_loop(0, group // STEP, inflow_step, 0)

        wait_group(0, group - 1)
        inflow_group(0)
        for j in range(1, GROUPS):
            wait_group(j, group)
            inflow_group(j)
        sent = pl.ds(0, devices - 1)
        pltpu.make_async_remote_copy(
            src_ref=send2.at[n, sent],
            dst_ref=recv2.at[n, sent],
            send_sem=send2_sem.at[n],
            recv_sem=recv2_sem.at[n, 0],
            device_id=place(me),
            device_id_type=MESH,
        ).wait_send()

        for c in range(4):
            at = slice(c * cell_rows, (c + 1) * cell_rows)
            forcing[at, :] = forcing[at, :] - total4[:, c * 128 : (c + 1) * 128]

        def first_sweep(c, z, at):
            value = forcing[at, :] * factor[at, :]
            corr[0, at, :] = value
            return value

        packed = for_tiles(first_sweep)
        for k in range(1, SWEEPS):
            now, later = corr.at[(k - 1) % 2], corr.at[k % 2]
            send_rims(turn + k, now, packed)
            wait_rims(turn + k)
            mask_rims(turn + k)

            def sweep(c, z, at):
                _, near = neighbours(turn + k, now, c, z, at)
                value = (forcing[at, :] + near) * factor[at, :]
                if k < SWEEPS - 1:
                    later[at, :] = value
                    return value
                state_out[at, :] = state_out[at, :] - value

            packed = for_tiles(sweep)
        return carry

    lax.fori_loop(0, NEWTON, newton, 0)


def on_device(n_gx, n_gy, state_init, right_side, rock_type, trans_table, perf_cells, seg_slot, seg_inverse):
    channels, layers, rows, columns = state_init.shape
    devices = n_gx * n_gy
    wells, segments = seg_slot.shape
    cell_rows = layers * rows
    tiles = channels * layers
    field = (channels * cell_rows, columns)
    vmem = pl.BlockSpec(memory_space=pltpu.VMEM)
    hbm = pl.BlockSpec(memory_space=pl.ANY)
    smem = pl.BlockSpec(memory_space=pltpu.SMEM)
    turns = NEWTON * SWEEPS
    dma = pltpu.SemaphoreType.DMA
    state, rates = pl.pallas_call(
        functools.partial(kernel, n_gx, n_gy, layers, wells),
        out_shape=(
            jax.ShapeDtypeStruct(field, F32),
            jax.ShapeDtypeStruct((channels * wells, segments), F32),
        ),
        in_specs=[hbm, hbm, hbm, smem, hbm, hbm, hbm],
        out_specs=(vmem, vmem),
        scratch_shapes=[
            pltpu.VMEM(field, F32),
            pltpu.VMEM((cell_rows, columns), jnp.int32),
            pltpu.VMEM((devices, perf_cells.shape[2]), jnp.int32),
            pltpu.VMEM((wells, segments), jnp.int32),
            pltpu.VMEM(seg_inverse.shape, F32),
            dma((6,)),
            pltpu.VMEM(field, F32),
            pltpu.VMEM(field, F32),
            pltpu.VMEM(field, F32),
            pltpu.VMEM((2,) + field, F32),
            pltpu.VMEM((channels, cell_rows, 256), BF16),
            pltpu.VMEM((NEWTON, devices, channels, 128), F32),
            pltpu.VMEM((NEWTON, devices, channels, 128), F32),
            pltpu.VMEM((channels * devices, 256), BF16),
            pltpu.VMEM((2, channels * wells, 128), F32),
            pltpu.VMEM((NEWTON, devices, channels, 128), F32),
            pltpu.VMEM((NEWTON, devices, channels, 128), F32),
            pltpu.VMEM((channels * devices, 128), F32),
            pltpu.VMEM((cell_rows, channels * 128), F32),
            pltpu.VMEM((segments, segments), F32),
            pltpu.VMEM((turns, 2, tiles, 128), F32),
            pltpu.VMEM((turns, 2, tiles, 128), F32),
            pltpu.VMEM((turns, 2, 8, 128), F32),
            pltpu.VMEM((turns, 2, 8, 128), F32),
            dma((NEWTON,)),
            dma((NEWTON,)),
            dma((NEWTON,)),
            dma((NEWTON, GROUPS)),
            dma((turns, 4)),
            dma((turns, 4)),
        ],
        compiler_params=pltpu.CompilerParams(
            collective_id=0, has_side_effects=True, vmem_limit_bytes=62 * 1024 * 1024
        ),
        name="newton",
    )(
        state_init.reshape(field),
        right_side.reshape(field),
        rock_type.reshape(cell_rows, columns),
        trans_table,
        perf_cells.reshape(devices, perf_cells.shape[2]),
        seg_slot,
        seg_inverse,
    )
    return state.reshape(state_init.shape), rates.reshape(channels, wells, segments)


def solution(mesh):
    in_specs = (
        P(None, None, "gx", "gy"),
        P(None, None, "gx", "gy"),
        P(None, "gx", "gy"),
        P(),
        P(("gx", "gy"), None, None),
        P(("gx", "gy"), None),
        P(None, None, ("gx", "gy"), None),
    )
    out_specs = (P(None, None, "gx", "gy"), P(None, ("gx", "gy"), None))
    return jax.shard_map(
        functools.partial(on_device, mesh.shape["gx"], mesh.shape["gy"]),
        mesh=mesh,
        in_specs=in_specs,
        out_specs=out_specs,
        check_vma=False,
    )
```

```python
import functools

import jax
import jax.numpy as jnp
from jax import lax
from jax.experimental import pallas as pl
from jax.experimental.pallas import tpu as pltpu
from jax.sharding import PartitionSpec as P

NEWTON = 2
SWEEPS = 4
GROUPS = 2
STEP = 16
WELLS_STEP = 8
CHUNK = 4
F32 = jnp.float32
BF16 = jnp.bfloat16
MESH = pl.DeviceIdType.MESH


def halves(x):
    high = x.astype(BF16)
    return high, (x - high.astype(F32)).astype(BF16)


def onehot(size, index):
    rows = lax.broadcasted_iota(jnp.int32, (size, index.shape[1]), 0)
    return jnp.where(rows == index, 1.0, 0.0).astype(BF16)


def kernel(
    n_gx, n_gy, layers, wells,
    state_in, right_in, rock_in, table, cells_in, slots_in, inverse_in,
    state_out, rates_out,
    right, rock, cells, slots, inverse, load_sem,
    coeff, forcing, factor, corr, split, send1, recv1, split2, rows, send2, recv2, total3, total4, decay,
    xs, xr, ys, yr,
    send1_sem, recv1_sem, send2_sem, recv2_sem, rim_send, rim_recv,
):
    gx, gy = lax.axis_index("gx"), lax.axis_index("gy")
    devices = n_gx * n_gy
    me = gx * n_gy + gy
    cell_rows = layers * 8
    tiles = 4 * layers
    group = devices // GROUPS
    my_group = lax.div(me, group)

    def place(device):
        return (lax.div(device, n_gy), lax.rem(device, n_gy))

    loads = [
        pltpu.make_async_copy(source, target, load_sem.at[k])
        for k, (source, target) in enumerate(
            (
                (rock_in, rock),
                (state_in, state_out),
                (cells_in, cells),
                (right_in, right),
                (slots_in, slots),
                (inverse_in, inverse),
            )
        )
    ]
    for load in loads:
        load.start()

    barrier = pltpu.get_barrier_semaphore()

    def greet(step, carry):
        pl.semaphore_signal(
            barrier, inc=1, device_id=place(lax.rem(me + step, devices)), device_id_type=MESH
        )
        return carry

    lax.fori_loop(1, devices, greet, 0)

    loads[0].wait()

    def coefficients(i, inner):
        at = pl.ds(pl.multiple_of(i * 8, 8), 8)
        kinds = rock[at, :]
        picked = [kinds == kind for kind in range(8)]
        for c in range(4):
            value = jnp.full((8, 128), 6.0, F32)
            for kind in range(8):
                value = value + jnp.where(picked[kind], table[c, kind], 0.0)
            coeff[pl.ds(pl.multiple_of(c * cell_rows + i * 8, 8), 8), :] = value
        return inner

    lax.fori_loop(0, layers, coefficients, 0, unroll=2)
    first = lax.broadcasted_iota(jnp.int32, decay.shape, 0)
    second = lax.broadcasted_iota(jnp.int32, decay.shape, 1)
    gap = (second - first).astype(F32)
    decay[...] = jnp.where(
        gap >= 0, 0.3 * jnp.exp(jnp.maximum(gap, 0.0) * -0.10536051565782628), 0.0
    )
    for load in loads[1:]:
        load.wait()

    lane = lax.broadcasted_iota(jnp.int32, (8, 128), 1)
    sub = lax.broadcasted_iota(jnp.int32, (8, 128), 0)

    def rim_copies(turn, c):
        right_x = (lax.rem(gx + 1, n_gx), gy)
        left_x = (lax.rem(gx + n_gx - 1, n_gx), gy)
        right_y = (gx, lax.rem(gy + 1, n_gy))
        left_y = (gx, lax.rem(gy + n_gy - 1, n_gy))
        mine = pl.ds(pl.multiple_of(c * layers, layers), layers)
        plan = (
            (xs.at[turn, 1, mine], xr.at[turn, 0, mine], right_x),
            (xs.at[turn, 0, mine], xr.at[turn, 1, mine], left_x),
            (ys.at[turn, c], yr.at[turn, c, 0], right_y),
            (ys.at[turn, c], yr.at[turn, c, 1], left_y),
        )
        return [
            pltpu.make_async_remote_copy(
                src_ref=src,
                dst_ref=dst,
                send_sem=rim_send.at[turn, c, k],
                recv_sem=rim_recv.at[turn, c, k],
                device_id=target,
                device_id_type=MESH,
            )
            for k, (src, dst, target) in enumerate(plan)
        ]

    def tile_of(c, z):
        return pl.ds(pl.multiple_of(c * cell_rows + z * 8, 8), 8)

    def pack(z, value, packed):
        return jnp.where((lane >> 1) == z, pltpu.roll(value, 2 * z + 1, axis=1), packed)

    def send_rims(turn, c, field, packed):
        mine = pl.ds(pl.multiple_of(c * layers, layers), layers)
        xs[turn, 0, mine, :] = field[pl.ds(c * cell_rows, layers, stride=8), :]
        xs[turn, 1, mine, :] = field[pl.ds(c * cell_rows + 7, layers, stride=8), :]
        ys[turn, c] = packed
        for copy in rim_copies(turn, c):
            copy.start()

    def open_rims(turn, c):
        for copy in rim_copies(turn, c):
            copy.wait()
        mine = pl.ds(pl.multiple_of(c * layers, layers), layers)
        xr[turn, 0, mine, :] = jnp.where(gx == 0, 0.0, xr[turn, 0, mine, :])
        xr[turn, 1, mine, :] = jnp.where(gx == n_gx - 1, 0.0, xr[turn, 1, mine, :])
        low = jnp.where(gy == 0, 0.0, yr[turn, c, 0])
        high = jnp.where(gy == n_gy - 1, 0.0, yr[turn, c, 1])
        return jnp.where((lane & 1) == 0, low, pltpu.roll(high, 126, axis=1))

    def neighbours(turn, field, c, z, columns):
        value = field[tile_of(c, z), :]
        row = c * layers + z
        column = pltpu.roll(columns, 128 - 2 * z, axis=1) if z else columns
        x_low = jnp.broadcast_to(xr[turn, 0, pl.ds(row, 1), :], (8, 128))
        x_high = jnp.broadcast_to(xr[turn, 1, pl.ds(row, 1), :], (8, 128))
        total = jnp.where(sub == 0, x_low, pltpu.roll(value, 1, axis=0))
        total = total + jnp.where(sub == 7, x_high, pltpu.roll(value, 7, axis=0))
        total = total + jnp.where(lane == 0, column, pltpu.roll(value, 1, axis=1))
        total = total + jnp.where(lane == 127, column, pltpu.roll(value, 127, axis=1))
        if z > 0:
            total = total + field[tile_of(c, z - 1), :]
        if z < layers - 1:
            total = total + field[tile_of(c, z + 1), :]
        return value, total

    no_columns = jnp.zeros((8, 128), F32)

    def split_channel(c):
        high, low = halves(state_out[pl.ds(pl.multiple_of(c * cell_rows, cell_rows), cell_rows), :])
        split[c, :, 0:128] = high
        split[c, :, 128:256] = low

    def split_first(c, carry):
        split_channel(c)
        return carry

    lax.fori_loop(0, 4, split_first, 0)

    def block_copy(source, target, source_slot, target_slot, device, send_sem, recv_sem):
        return pltpu.make_async_remote_copy(
            src_ref=source.at[source_slot],
            dst_ref=target.at[target_slot],
            send_sem=send_sem,
            recv_sem=recv_sem,
            device_id=place(device),
            device_id_type=MESH,
        )

    def newton(n, carry):
        turn = n * SWEEPS

        def gather_pair(pair):
            index = jnp.concatenate([cells[pl.ds(2 * pair + k, 1), :] for k in range(2)], axis=1)
            pick = onehot(128, index & 127)
            pick = jnp.concatenate([pick, pick], axis=0)
            wanted = lax.broadcasted_iota(jnp.int32, (cell_rows, 256), 0) == (index >> 7)
            found = []
            for c in range(4):
                value = jnp.dot(split[c], pick, preferred_element_type=F32)
                found.append(jnp.sum(jnp.where(wanted, value, 0.0), axis=0, keepdims=True))
            found = jnp.concatenate(found, axis=0)
            return found[:, :128], found[:, 128:]

        my_pair = lax.div(me, 2)
        pairs = devices // 2

        def pair_of(chunk, k):
            return lax.rem(my_pair + 1 + chunk * CHUNK + k, pairs)

        def gather_chunk(chunk):
            for k in range(CHUNK):
                pair = pair_of(chunk, k)
                for side, block in enumerate(gather_pair(pair)):
                    send1[n, 2 * pair + side] = block

        def send_block(target):
            block_copy(send1.at[n], recv1.at[n], target, me, target, send1_sem.at[n], recv1_sem.at[n]).start()

        def send_chunk(chunk, count=CHUNK):
            for k in range(count):
                for side in range(2):
                    send_block(2 * pair_of(chunk, k) + side)

        chunks = pairs // CHUNK
        early = chunks // 2

        def early_step(chunk, inner):
            gather_chunk(chunk)
            return inner

        lax.fori_loop(0, early, early_step, 0)

        @pl.when(n == 0)
        def _():
            pl.semaphore_wait(barrier, devices - 1)

            def first_rims(c, inner):
                packed = no_columns
                for z in range(layers):
                    packed = pack(z, state_out[tile_of(c, z), :], packed)
                send_rims(turn, c, state_out, packed)
                return inner

            lax.fori_loop(0, 4, first_rims, 0)

        def late_step(step, inner):
            send_chunk(2 * step)
            send_chunk(2 * step + 1)
            gather_chunk(early + step)
            return inner

        lax.fori_loop(0, chunks - early - 1, late_step, 0)
        send_chunk(chunks - 2)
        gather_chunk(chunks - 1)
        send_chunk(chunks - 1, CHUNK - 1)
        send_block(4 * my_pair + 1 - me)
        recv1[n, me] = send1[n, me]

        def base(c, inner):
            columns = open_rims(turn, c)
            for z in range(layers):
                at = tile_of(c, z)
                value, near = neighbours(turn, state_out, c, z, columns)
                square = value * value
                forcing[at, :] = coeff[at, :] * value - near + 0.1 * square * value - right[at, :]
                factor[at, :] = 1.0 / (coeff[at, :] + 0.3 * square)
            return inner

        lax.fori_loop(0, 4, base, 0)

        all_blocks = pl.ds(0, devices - 1)
        arrived = pltpu.make_async_remote_copy(
            src_ref=send1.at[n, all_blocks],
            dst_ref=recv1.at[n, all_blocks],
            send_sem=send1_sem.at[n],
            recv_sem=recv1_sem.at[n],
            device_id=place(me),
            device_id_type=MESH,
        )
        arrived.wait_recv()

        high, low = halves(recv1[n].reshape(4 * devices, 128))
        split2[:, 0:128] = high
        split2[:, 128:256] = low
        quarter = lax.broadcasted_iota(jnp.int32, (4 * devices, 256), 0) >> 2

        def owner_gather(w, inner):
            index = slots[pl.ds(w, 1), :]
            pick = onehot(128, index & 127)
            pick = jnp.concatenate([pick, pick], axis=0)
            value = jnp.dot(split2[...], pick, preferred_element_type=F32)
            value = jnp.where(quarter == (index >> 7), value, 0.0)
            value = jnp.sum(value.reshape(devices // 2, 8, 256), axis=0)
            value = value[0:4] + value[4:8]
            rows[0, pl.ds(w, 4, stride=wells), :] = value[:, :128]
            rows[1, pl.ds(w, 4, stride=wells), :] = value[:, 128:]
            return inner

        lax.fori_loop(0, wells, owner_gather, 0, unroll=4)
        flows = []
        for i in range(4):
            sides = []
            for half in range(2):
                at = slice(half * 128, half * 128 + 128)
                flow = inverse[i, 0, :, at] * rows[half, 0:wells, :]
                for j in range(1, 4):
                    flow = flow + inverse[i, j, :, at] * rows[half, j * wells : (j + 1) * wells, :]
                sides.append(flow)
            flows.append(jnp.concatenate(sides, axis=1))
        rates = jnp.dot(
            jnp.concatenate(flows, axis=0),
            decay[...],
            precision=lax.Precision.HIGHEST,
            preferred_element_type=F32,
        )
        rates_out[...] = rates
        rows[0] = rates[:, :128]
        rows[1] = rates[:, 128:]
        total3[...] = jnp.zeros_like(total3)

        def group_start(j):
            return lax.rem(my_group + j, GROUPS) * group

        def owner_scatter(j, step):
            first_well = step * WELLS_STEP
            width = WELLS_STEP * 256
            index = jnp.concatenate([slots[pl.ds(first_well + k, 1), :] for k in range(WELLS_STEP)], axis=1)
            rate = jnp.concatenate(
                [rows[half, pl.ds(first_well + k, 4, stride=wells), :] for k in range(WELLS_STEP) for half in range(2)],
                axis=1,
            )
            pick = onehot(128, index & 127)
            wanted = (lax.broadcasted_iota(jnp.int32, (4 * group, width), 0) >> 2) == (index >> 7) - group_start(j)
            parts = []
            for half in halves(jnp.concatenate([rate, rate], axis=0)):
                spread = jnp.broadcast_to(half.astype(F32)[None], (group // 2, 8, width))
                parts.append(jnp.where(wanted, spread.reshape(4 * group, width), 0.0).astype(BF16))
            total3[j] += lax.dot_general(
                jnp.concatenate(parts, axis=1),
                jnp.concatenate([pick, pick], axis=1),
                (((1,), (1,)), ((), ())),
                preferred_element_type=F32,
            )

        def return_block(j, step):
            target = group_start(j) + lax.rem(me + step, group)
            block_copy(send2.at[n], recv2.at[n], target, me, target, send2_sem.at[n], recv2_sem.at[n, j]).start()

        well_steps = wells // WELLS_STEP
        each = group // well_steps

        def own_half(step, inner):
            owner_scatter(0, step)
            return inner

        lax.fori_loop(0, well_steps, own_half, 0)
        send2[n, pl.ds(group_start(0), group)] = total3[0].reshape(group, 4, 128)
        recv2[n, me] = send2[n, me]

        def other_half(step, inner):
            for k in range(each - 1):
                return_block(0, 1 + step * each + k)

            @pl.when(step < well_steps - 1)
            def _():
                return_block(0, each + step * each)

            owner_scatter(1, step)
            return inner

        lax.fori_loop(0, well_steps, other_half, 0)
        send2[n, pl.ds(group_start(1), group)] = total3[1].reshape(group, 4, 128)
        arrived.wait_send()

        total4[...] = jnp.zeros_like(total4)

        def wait_group(j, count):
            some = pl.ds(0, count)
            pltpu.make_async_remote_copy(
                src_ref=send2.at[n, some],
                dst_ref=recv2.at[n, some],
                send_sem=send2_sem.at[n],
                recv_sem=recv2_sem.at[n, j],
                device_id=place(me),
                device_id_type=MESH,
            ).wait_recv()

        def inflow_group(j):
            start = group_start(j)

            def inflow_step(step, inner):
                if j == 0:
                    for k in range(STEP):
                        return_block(1, step * STEP + k)
                owner = start + step * STEP
                index = jnp.concatenate([cells[pl.ds(owner + k, 1), :] for k in range(STEP)], axis=1)
                value = jnp.concatenate([recv2[n, owner + k] for k in range(STEP)], axis=1)
                lanes = onehot(128, index & 127)
                pick = onehot(cell_rows, index >> 7)
                pick = jnp.concatenate([pick, pick], axis=1)
                high, low = halves(value)
                spread = jnp.concatenate(
                    [
                        jnp.concatenate([lanes * high[c : c + 1], lanes * low[c : c + 1]], axis=1)
                        for c in range(4)
                    ],
                    axis=0,
                )
                total4[...] += lax.dot_general(
                    pick, spread, (((1,), (1,)), ((), ())), preferred_element_type=F32
                )
                return inner

            lax.fori_loop(0, group // STEP, inflow_step, 0)

        wait_group(0, group - 1)
        inflow_group(0)
        for j in range(1, GROUPS):
            wait_group(j, group)
            inflow_group(j)
        sent = pl.ds(0, devices - 1)
        pltpu.make_async_remote_copy(
            src_ref=send2.at[n, sent],
            dst_ref=recv2.at[n, sent],
            send_sem=send2_sem.at[n],
            recv_sem=recv2_sem.at[n, 0],
            device_id=place(me),
            device_id_type=MESH,
        ).wait_send()

        def first_sweep(c, inner):
            packed = no_columns
            for z in range(layers):
                at = tile_of(c, z)
                inflow = total4[z * 8 : z * 8 + 8, pl.ds(pl.multiple_of(c * 128, 128), 128)]
                value = forcing[at, :] - inflow
                forcing[at, :] = value
                value = value * factor[at, :]
                corr[0, at, :] = value
                packed = pack(z, value, packed)
            send_rims(turn + 1, c, corr.at[0], packed)
            return inner

        lax.fori_loop(0, 4, first_sweep, 0)
        for k in range(1, SWEEPS):
            now, later = corr.at[(k - 1) % 2], corr.at[k % 2]

            def sweep(c, inner):
                columns = open_rims(turn + k, c)
                packed = no_columns
                for z in range(layers):
                    at = tile_of(c, z)
                    _, near = neighbours(turn + k, now, c, z, columns)
                    value = (forcing[at, :] + near) * factor[at, :]
                    if k < SWEEPS - 1:
                        later[at, :] = value
                    else:
                        value = state_out[at, :] - value
                        state_out[at, :] = value
                    packed = pack(z, value, packed)
                if k < SWEEPS - 1:
                    send_rims(turn + k + 1, c, later, packed)
                else:

                    @pl.when(n < NEWTON - 1)
                    def _():
                        send_rims(turn + SWEEPS, c, state_out, packed)
                        split_channel(c)

                return inner

            lax.fori_loop(0, 4, sweep, 0)
        return carry

    lax.fori_loop(0, NEWTON, newton, 0)


def on_device(n_gx, n_gy, state_init, right_side, rock_type, trans_table, perf_cells, seg_slot, seg_inverse):
    channels, layers, rows, columns = state_init.shape
    devices = n_gx * n_gy
    wells, segments = seg_slot.shape
    cell_rows = layers * rows
    tiles = channels * layers
    field = (channels * cell_rows, columns)
    vmem = pl.BlockSpec(memory_space=pltpu.VMEM)
    hbm = pl.BlockSpec(memory_space=pl.ANY)
    smem = pl.BlockSpec(memory_space=pltpu.SMEM)
    turns = NEWTON * SWEEPS
    dma = pltpu.SemaphoreType.DMA
    state, rates = pl.pallas_call(
        functools.partial(kernel, n_gx, n_gy, layers, wells),
        out_shape=(
            jax.ShapeDtypeStruct(field, F32),
            jax.ShapeDtypeStruct((channels * wells, segments), F32),
        ),
        in_specs=[hbm, hbm, hbm, smem, hbm, hbm, hbm],
        out_specs=(vmem, vmem),
        scratch_shapes=[
            pltpu.VMEM(field, F32),
            pltpu.VMEM((cell_rows, columns), jnp.int32),
            pltpu.VMEM((devices, perf_cells.shape[2]), jnp.int32),
            pltpu.VMEM((wells, segments), jnp.int32),
            pltpu.VMEM(seg_inverse.shape, F32),
            dma((6,)),
            pltpu.VMEM(field, F32),
            pltpu.VMEM(field, F32),
            pltpu.VMEM(field, F32),
            pltpu.VMEM((2,) + field, F32),
            pltpu.VMEM((channels, cell_rows, 256), BF16),
            pltpu.VMEM((NEWTON, devices, channels, 128), F32),
            pltpu.VMEM((NEWTON, devices, channels, 128), F32),
            pltpu.VMEM((channels * devices, 256), BF16),
            pltpu.VMEM((2, channels * wells, 128), F32),
            pltpu.VMEM((NEWTON, devices, channels, 128), F32),
            pltpu.VMEM((NEWTON, devices, channels, 128), F32),
            pltpu.VMEM((GROUPS, channels * devices // GROUPS, 128), F32),
            pltpu.VMEM((cell_rows, channels * 128), F32),
            pltpu.VMEM((segments, segments), F32),
            pltpu.VMEM((turns, 2, tiles, 128), F32),
            pltpu.VMEM((turns, 2, tiles, 128), F32),
            pltpu.VMEM((turns, channels, 8, 128), F32),
            pltpu.VMEM((turns, channels, 2, 8, 128), F32),
            dma((NEWTON,)),
            dma((NEWTON,)),
            dma((NEWTON,)),
            dma((NEWTON, GROUPS)),
            dma((turns, channels, 4)),
            dma((turns, channels, 4)),
        ],
        compiler_params=pltpu.CompilerParams(
            collective_id=0, has_side_effects=True, vmem_limit_bytes=62 * 1024 * 1024
        ),
        name="newton",
    )(
        state_init.reshape(field),
        right_side.reshape(field),
        rock_type.reshape(cell_rows, columns),
        trans_table,
        perf_cells.reshape(devices, perf_cells.shape[2]),
        seg_slot,
        seg_inverse,
    )
    return state.reshape(state_init.shape), rates.reshape(channels, wells, segments)


def solution(mesh):
    in_specs = (
        P(None, None, "gx", "gy"),
        P(None, None, "gx", "gy"),
        P(None, "gx", "gy"),
        P(),
        P(("gx", "gy"), None, None),
        P(("gx", "gy"), None),
        P(None, None, ("gx", "gy"), None),
    )
    out_specs = (P(None, None, "gx", "gy"), P(None, ("gx", "gy"), None))
    return jax.shard_map(
        functools.partial(on_device, mesh.shape["gx"], mesh.shape["gy"]),
        mesh=mesh,
        in_specs=in_specs,
        out_specs=out_specs,
        check_vma=False,
    )
```

```python
import functools

import jax
import jax.numpy as jnp
from jax import lax
from jax.experimental import pallas as pl
from jax.experimental.pallas import tpu as pltpu
from jax.sharding import PartitionSpec as P

NEWTON = 2
SWEEPS = 4
PLANES = 4
PLANE_ORDER = (0, 1, 3, 2)
CHUNK_ORDER = (10, 9, 11, 6, 14, 5, 7, 13, 15, 8, 2, 4, 12, 1, 3, 0)
WELLS_STEP = 8
CHUNK = 4
F32 = jnp.float32
BF16 = jnp.bfloat16
MESH = pl.DeviceIdType.MESH


def halves(x):
    high = x.astype(BF16)
    return high, (x - high.astype(F32)).astype(BF16)


def onehot(size, index):
    rows = lax.broadcasted_iota(jnp.int32, (size, index.shape[1]), 0)
    return jnp.where(rows == index, 1.0, 0.0).astype(BF16)


def kernel(
    n_gx, n_gy, layers, wells,
    state_in, right_in, rock_in, table, cells_in, slots_in, inverse_in,
    state_out, rates_out,
    right, rock, cells, slots, inverse, load_sem,
    coeff, forcing, factor, corr, split, send1, recv1, split2, rows, send2, recv2, total3, total4, decay,
    xs, xr, ys, yr,
    send1_sem, recv1_sem, send2_sem, recv2_sem, rim_send, rim_recv,
):
    gx, gy = lax.axis_index("gx"), lax.axis_index("gy")
    devices = n_gx * n_gy
    me = gx * n_gy + gy
    cell_rows = layers * 8
    tiles = 4 * layers
    group = devices // PLANES
    my_group = lax.div(me, group)

    def place(device):
        return (lax.div(device, n_gy), lax.rem(device, n_gy))

    loads = [
        pltpu.make_async_copy(source, target, load_sem.at[k])
        for k, (source, target) in enumerate(
            (
                (rock_in, rock),
                (state_in, state_out),
                (cells_in, cells),
                (right_in, right),
                (slots_in, slots),
                (inverse_in, inverse),
            )
        )
    ]
    for load in loads:
        load.start()

    barrier = pltpu.get_barrier_semaphore()

    def greet(step, carry):
        pl.semaphore_signal(
            barrier, inc=1, device_id=place(lax.rem(me + step, devices)), device_id_type=MESH
        )
        return carry

    lax.fori_loop(1, devices, greet, 0)

    loads[0].wait()

    def coefficients(i, inner):
        at = pl.ds(pl.multiple_of(i * 8, 8), 8)
        kinds = rock[at, :]
        picked = [kinds == kind for kind in range(8)]
        for c in range(4):
            value = jnp.full((8, 128), 6.0, F32)
            for kind in range(8):
                value = value + jnp.where(picked[kind], table[c, kind], 0.0)
            coeff[pl.ds(pl.multiple_of(c * cell_rows + i * 8, 8), 8), :] = value
        return inner

    lax.fori_loop(0, layers, coefficients, 0, unroll=2)
    first = lax.broadcasted_iota(jnp.int32, decay.shape, 0)
    second = lax.broadcasted_iota(jnp.int32, decay.shape, 1)
    gap = (second - first).astype(F32)
    decay[...] = jnp.where(
        gap >= 0, 0.3 * jnp.exp(jnp.maximum(gap, 0.0) * -0.10536051565782628), 0.0
    )
    for load in loads[1:]:
        load.wait()

    lane = lax.broadcasted_iota(jnp.int32, (8, 128), 1)
    sub = lax.broadcasted_iota(jnp.int32, (8, 128), 0)

    def rim_copies(turn, c):
        right_x = (lax.rem(gx + 1, n_gx), gy)
        left_x = (lax.rem(gx + n_gx - 1, n_gx), gy)
        right_y = (gx, lax.rem(gy + 1, n_gy))
        left_y = (gx, lax.rem(gy + n_gy - 1, n_gy))
        mine = pl.ds(pl.multiple_of(c * layers, layers), layers)
        plan = (
            (xs.at[turn, 1, mine], xr.at[turn, 0, mine], right_x),
            (xs.at[turn, 0, mine], xr.at[turn, 1, mine], left_x),
            (ys.at[turn, c], yr.at[turn, c, 0], right_y),
            (ys.at[turn, c], yr.at[turn, c, 1], left_y),
        )
        return [
            pltpu.make_async_remote_copy(
                src_ref=src,
                dst_ref=dst,
                send_sem=rim_send.at[turn, c, k],
                recv_sem=rim_recv.at[turn, c, k],
                device_id=target,
                device_id_type=MESH,
            )
            for k, (src, dst, target) in enumerate(plan)
        ]

    def tile_of(c, z):
        return pl.ds(pl.multiple_of(c * cell_rows + z * 8, 8), 8)

    def pack(z, value, packed):
        return jnp.where((lane >> 1) == z, pltpu.roll(value, 2 * z + 1, axis=1), packed)

    def send_rims(turn, c, field, packed):
        mine = pl.ds(pl.multiple_of(c * layers, layers), layers)
        xs[turn, 0, mine, :] = field[pl.ds(c * cell_rows, layers, stride=8), :]
        xs[turn, 1, mine, :] = field[pl.ds(c * cell_rows + 7, layers, stride=8), :]
        ys[turn, c] = packed
        for copy in rim_copies(turn, c):
            copy.start()

    def open_rims(turn, c):
        for copy in rim_copies(turn, c):
            copy.wait()
        mine = pl.ds(pl.multiple_of(c * layers, layers), layers)
        xr[turn, 0, mine, :] = jnp.where(gx == 0, 0.0, xr[turn, 0, mine, :])
        xr[turn, 1, mine, :] = jnp.where(gx == n_gx - 1, 0.0, xr[turn, 1, mine, :])
        low = jnp.where(gy == 0, 0.0, yr[turn, c, 0])
        high = jnp.where(gy == n_gy - 1, 0.0, yr[turn, c, 1])
        return jnp.where((lane & 1) == 0, low, pltpu.roll(high, 126, axis=1))

    def neighbours(turn, field, c, z, columns):
        value = field[tile_of(c, z), :]
        row = c * layers + z
        column = pltpu.roll(columns, 128 - 2 * z, axis=1) if z else columns
        x_low = jnp.broadcast_to(xr[turn, 0, pl.ds(row, 1), :], (8, 128))
        x_high = jnp.broadcast_to(xr[turn, 1, pl.ds(row, 1), :], (8, 128))
        total = jnp.where(sub == 0, x_low, pltpu.roll(value, 1, axis=0))
        total = total + jnp.where(sub == 7, x_high, pltpu.roll(value, 7, axis=0))
        total = total + jnp.where(lane == 0, column, pltpu.roll(value, 1, axis=1))
        total = total + jnp.where(lane == 127, column, pltpu.roll(value, 127, axis=1))
        if z > 0:
            total = total + field[tile_of(c, z - 1), :]
        if z < layers - 1:
            total = total + field[tile_of(c, z + 1), :]
        return value, total

    no_columns = jnp.zeros((8, 128), F32)

    def split_channel(c):
        high, low = halves(state_out[pl.ds(pl.multiple_of(c * cell_rows, cell_rows), cell_rows), :])
        split[c, :, 0:128] = high
        split[c, :, 128:256] = low

    def split_first(c, carry):
        split_channel(c)
        return carry

    lax.fori_loop(0, 4, split_first, 0)

    def block_copy(source, target, source_slot, target_slot, device, send_sem, recv_sem):
        return pltpu.make_async_remote_copy(
            src_ref=source.at[source_slot],
            dst_ref=target.at[target_slot],
            send_sem=send_sem,
            recv_sem=recv_sem,
            device_id=place(device),
            device_id_type=MESH,
        )

    def newton(n, carry):
        turn = n * SWEEPS

        def gather_pair(pair):
            index = jnp.concatenate([cells[pl.ds(2 * pair + k, 1), :] for k in range(2)], axis=1)
            pick = onehot(128, index & 127)
            pick = jnp.concatenate([pick, pick], axis=0)
            wanted = lax.broadcasted_iota(jnp.int32, (cell_rows, 256), 0) == (index >> 7)
            found = []
            for c in range(4):
                value = jnp.dot(split[c], pick, preferred_element_type=F32)
                found.append(jnp.sum(jnp.where(wanted, value, 0.0), axis=0, keepdims=True))
            found = jnp.concatenate(found, axis=0)
            return found[:, :128], found[:, 128:]


        my_pair = lax.div(me, 2)
        pairs = devices // 2

        def pair_of(chunk, k):
            away = 0
            for i, code in enumerate(CHUNK_ORDER):
                away = jnp.where(chunk == i, code, away)
            chip_x = lax.rem(lax.div(gx, 2) + lax.div(away, 4), 4)
            core = lax.rem(gx + 1 - k // 2, 2)
            chip_z = lax.rem(lax.div(gy, 4) + lax.rem(away, 4), 4)
            half_y = lax.rem(lax.div(gy, 2) + 1 - k % 2, 2)
            return (2 * chip_x + core) * (n_gy // 2) + chip_z * 2 + half_y

        def gather_chunk(chunk):
            for k in range(CHUNK):
                pair = pair_of(chunk, k)
                for side, block in enumerate(gather_pair(pair)):
                    send1[n, 2 * pair + side] = block

        def send_block(target):
            block_copy(send1.at[n], recv1.at[n], target, me, target, send1_sem.at[n], recv1_sem.at[n]).start()

        def send_chunk(chunk, count=CHUNK):
            for k in range(count):
                for side in range(2):
                    send_block(2 * pair_of(chunk, k) + side)

        chunks = pairs // CHUNK
        early = chunks // 2

        def early_step(chunk, inner):
            gather_chunk(chunk)
            return inner

        lax.fori_loop(0, early, early_step, 0)

        @pl.when(n == 0)
        def _():
            pl.semaphore_wait(barrier, devices - 1)

            def first_rims(c, inner):
                packed = no_columns
                for z in range(layers):
                    packed = pack(z, state_out[tile_of(c, z), :], packed)
                send_rims(turn, c, state_out, packed)
                return inner

            lax.fori_loop(0, 4, first_rims, 0)

        def late_step(step, inner):
            send_chunk(2 * step)
            send_chunk(2 * step + 1)
            gather_chunk(early + step)
            return inner

        lax.fori_loop(0, chunks - early - 1, late_step, 0)
        send_chunk(chunks - 2)
        gather_chunk(chunks - 1)
        send_chunk(chunks - 1, CHUNK - 1)
        send_block(4 * my_pair + 1 - me)
        recv1[n, me] = send1[n, me]

        def base(c, inner):
            columns = open_rims(turn, c)
            for z in range(layers):
                at = tile_of(c, z)
                value, near = neighbours(turn, state_out, c, z, columns)
                square = value * value
                forcing[at, :] = coeff[at, :] * value - near + 0.1 * square * value - right[at, :]
                factor[at, :] = 1.0 / (coeff[at, :] + 0.3 * square)
            return inner

        lax.fori_loop(0, 4, base, 0)

        all_blocks = pl.ds(0, devices - 1)
        arrived = pltpu.make_async_remote_copy(
            src_ref=send1.at[n, all_blocks],
            dst_ref=recv1.at[n, all_blocks],
            send_sem=send1_sem.at[n],
            recv_sem=recv1_sem.at[n],
            device_id=place(me),
            device_id_type=MESH,
        )
        arrived.wait_recv()

        high, low = halves(recv1[n].reshape(4 * devices, 128))
        split2[:, 0:128] = high
        split2[:, 128:256] = low
        quarter = lax.broadcasted_iota(jnp.int32, (4 * devices, 256), 0) >> 2

        def owner_gather(w, inner):
            index = slots[pl.ds(w, 1), :]
            pick = onehot(128, index & 127)
            pick = jnp.concatenate([pick, pick], axis=0)
            value = jnp.dot(split2[...], pick, preferred_element_type=F32)
            value = jnp.where(quarter == (index >> 7), value, 0.0)
            value = jnp.sum(value.reshape(devices // 2, 8, 256), axis=0)
            value = value[0:4] + value[4:8]
            rows[0, pl.ds(w, 4, stride=wells), :] = value[:, :128]
            rows[1, pl.ds(w, 4, stride=wells), :] = value[:, 128:]
            return inner

        lax.fori_loop(0, wells, owner_gather, 0, unroll=4)
        flows = []
        for i in range(4):
            sides = []
            for half in range(2):
                at = slice(half * 128, half * 128 + 128)
                flow = inverse[i, 0, :, at] * rows[half, 0:wells, :]
                for j in range(1, 4):
                    flow = flow + inverse[i, j, :, at] * rows[half, j * wells : (j + 1) * wells, :]
                sides.append(flow)
            flows.append(jnp.concatenate(sides, axis=1))
        rates = jnp.dot(
            jnp.concatenate(flows, axis=0),
            decay[...],
            precision=lax.Precision.HIGHEST,
            preferred_element_type=F32,
        )
        rates_out[...] = rates
        rows[0] = rates[:, :128]
        rows[1] = rates[:, 128:]
        total3[...] = jnp.zeros_like(total3)

        def plane_start(away):
            return lax.rem(my_group + away, PLANES) * group

        def owner_scatter(side, step):
            first_well = step * WELLS_STEP
            width = WELLS_STEP * 256
            index = jnp.concatenate([slots[pl.ds(first_well + k, 1), :] for k in range(WELLS_STEP)], axis=1)
            rate = jnp.concatenate(
                [rows[half, pl.ds(first_well + k, 4, stride=wells), :] for k in range(WELLS_STEP) for half in range(2)],
                axis=1,
            )
            pick = onehot(128, index & 127)
            row = lax.broadcasted_iota(jnp.int32, (8 * group, width), 0)
            near, far = (plane_start(PLANE_ORDER[2 * side + k]) for k in range(2))
            device = jnp.where(row < 4 * group, near, far - group) + (row >> 2)
            wanted = device == (index >> 7)
            parts = []
            for half in halves(jnp.concatenate([rate, rate], axis=0)):
                spread = jnp.broadcast_to(half.astype(F32)[None], (group, 8, width))
                parts.append(jnp.where(wanted, spread.reshape(8 * group, width), 0.0).astype(BF16))
            total3[side] += lax.dot_general(
                jnp.concatenate(parts, axis=1),
                jnp.concatenate([pick, pick], axis=1),
                (((1,), (1,)), ((), ())),
                preferred_element_type=F32,
            )

        for side in range(2):

            def owner_step(step, inner):
                owner_scatter(side, step)
                return inner

            lax.fori_loop(0, wells // WELLS_STEP, owner_step, 0)
            for k in range(2):
                j = 2 * side + k
                start = plane_start(PLANE_ORDER[j])
                send2[n, pl.ds(start, group)] = total3[side, 4 * group * k : 4 * group * (k + 1)].reshape(group, 4, 128)

                def return_step(step, inner):
                    target = start + lax.rem(me + step, group)
                    block_copy(
                        send2.at[n], recv2.at[n], target, me, target, send2_sem.at[n], recv2_sem.at[n, j]
                    ).start()
                    return inner

                lax.fori_loop(1 if j == 0 else 0, group, return_step, 0)
            if side == 0:
                recv2[n, me] = send2[n, me]
        arrived.wait_send()


        def wait_group(j, count):
            some = pl.ds(0, count)
            pltpu.make_async_remote_copy(
                src_ref=send2.at[n, some],
                dst_ref=recv2.at[n, some],
                send_sem=send2_sem.at[n],
                recv_sem=recv2_sem.at[n, j],
                device_id=place(me),
                device_id_type=MESH,
            ).wait_recv()

        for j in range(PLANES):
            wait_group(j, group - 1 if j == 0 else group)
            start = lax.rem(my_group + PLANES - PLANE_ORDER[j], PLANES) * group
            index = jnp.concatenate([cells[pl.ds(start + k, 1), :] for k in range(group)], axis=1)
            value = jnp.concatenate([recv2[n, start + k] for k in range(group)], axis=1)
            lanes = onehot(128, index & 127)
            pick = onehot(cell_rows, index >> 7)
            pick = jnp.concatenate([pick, pick], axis=1)
            high, low = halves(value)
            spread = jnp.concatenate(
                [
                    jnp.concatenate([lanes * high[c : c + 1], lanes * low[c : c + 1]], axis=1)
                    for c in range(4)
                ],
                axis=0,
            )
            found = lax.dot_general(pick, spread, (((1,), (1,)), ((), ())), preferred_element_type=F32)
            if j == 0:
                total4[...] = found
            else:
                total4[...] += found
        sent = pl.ds(0, devices - 1)
        pltpu.make_async_remote_copy(
            src_ref=send2.at[n, sent],
            dst_ref=recv2.at[n, sent],
            send_sem=send2_sem.at[n],
            recv_sem=recv2_sem.at[n, 0],
            device_id=place(me),
            device_id_type=MESH,
        ).wait_send()

        def first_sweep(c, inner):
            packed = no_columns
            for z in range(layers):
                at = tile_of(c, z)
                inflow = total4[z * 8 : z * 8 + 8, pl.ds(pl.multiple_of(c * 128, 128), 128)]
                value = forcing[at, :] - inflow
                forcing[at, :] = value
                value = value * factor[at, :]
                corr[0, at, :] = value
                packed = pack(z, value, packed)
            send_rims(turn + 1, c, corr.at[0], packed)
            return inner

        lax.fori_loop(0, 4, first_sweep, 0)
        for k in range(1, SWEEPS):
            now, later = corr.at[(k - 1) % 2], corr.at[k % 2]

            def sweep(c, inner):
                columns = open_rims(turn + k, c)
                packed = no_columns
                for z in range(layers):
                    at = tile_of(c, z)
                    _, near = neighbours(turn + k, now, c, z, columns)
                    value = (forcing[at, :] + near) * factor[at, :]
                    if k < SWEEPS - 1:
                        later[at, :] = value
                    else:
                        value = state_out[at, :] - value
                        state_out[at, :] = value
                    packed = pack(z, value, packed)
                if k < SWEEPS - 1:
                    send_rims(turn + k + 1, c, later, packed)
                else:

                    @pl.when(n < NEWTON - 1)
                    def _():
                        send_rims(turn + SWEEPS, c, state_out, packed)
                        split_channel(c)

                return inner

            lax.fori_loop(0, 4, sweep, 0)
        return carry

    lax.fori_loop(0, NEWTON, newton, 0)


def on_device(n_gx, n_gy, state_init, right_side, rock_type, trans_table, perf_cells, seg_slot, seg_inverse):
    channels, layers, rows, columns = state_init.shape
    devices = n_gx * n_gy
    wells, segments = seg_slot.shape
    cell_rows = layers * rows
    tiles = channels * layers
    field = (channels * cell_rows, columns)
    vmem = pl.BlockSpec(memory_space=pltpu.VMEM)
    hbm = pl.BlockSpec(memory_space=pl.ANY)
    smem = pl.BlockSpec(memory_space=pltpu.SMEM)
    turns = NEWTON * SWEEPS
    dma = pltpu.SemaphoreType.DMA
    state, rates = pl.pallas_call(
        functools.partial(kernel, n_gx, n_gy, layers, wells),
        out_shape=(
            jax.ShapeDtypeStruct(field, F32),
            jax.ShapeDtypeStruct((channels * wells, segments), F32),
        ),
        in_specs=[hbm, hbm, hbm, smem, hbm, hbm, hbm],
        out_specs=(vmem, vmem),
        scratch_shapes=[
            pltpu.VMEM(field, F32),
            pltpu.VMEM((cell_rows, columns), jnp.int32),
            pltpu.VMEM((devices, perf_cells.shape[2]), jnp.int32),
            pltpu.VMEM((wells, segments), jnp.int32),
            pltpu.VMEM(seg_inverse.shape, F32),
            dma((6,)),
            pltpu.VMEM(field, F32),
            pltpu.VMEM(field, F32),
            pltpu.VMEM(field, F32),
            pltpu.VMEM((2,) + field, F32),
            pltpu.VMEM((channels, cell_rows, 256), BF16),
            pltpu.VMEM((NEWTON, devices, channels, 128), F32),
            pltpu.VMEM((NEWTON, devices, channels, 128), F32),
            pltpu.VMEM((channels * devices, 256), BF16),
            pltpu.VMEM((2, channels * wells, 128), F32),
            pltpu.VMEM((NEWTON, devices, channels, 128), F32),
            pltpu.VMEM((NEWTON, devices, channels, 128), F32),
            pltpu.VMEM((2, channels * devices // 2, 128), F32),
            pltpu.VMEM((cell_rows, channels * 128), F32),
            pltpu.VMEM((segments, segments), F32),
            pltpu.VMEM((turns, 2, tiles, 128), F32),
            pltpu.VMEM((turns, 2, tiles, 128), F32),
            pltpu.VMEM((turns, channels, 8, 128), F32),
            pltpu.VMEM((turns, channels, 2, 8, 128), F32),
            dma((NEWTON,)),
            dma((NEWTON,)),
            dma((NEWTON,)),
            dma((NEWTON, PLANES)),
            dma((turns, channels, 4)),
            dma((turns, channels, 4)),
        ],
        compiler_params=pltpu.CompilerParams(
            collective_id=0, has_side_effects=True, vmem_limit_bytes=62 * 1024 * 1024
        ),
        name="newton",
    )(
        state_init.reshape(field),
        right_side.reshape(field),
        rock_type.reshape(cell_rows, columns),
        trans_table,
        perf_cells.reshape(devices, perf_cells.shape[2]),
        seg_slot,
        seg_inverse,
    )
    return state.reshape(state_init.shape), rates.reshape(channels, wells, segments)


def solution(mesh):
    in_specs = (
        P(None, None, "gx", "gy"),
        P(None, None, "gx", "gy"),
        P(None, "gx", "gy"),
        P(),
        P(("gx", "gy"), None, None),
        P(("gx", "gy"), None),
        P(None, None, ("gx", "gy"), None),
    )
    out_specs = (P(None, None, "gx", "gy"), P(None, ("gx", "gy"), None))
    return jax.shard_map(
        functools.partial(on_device, mesh.shape["gx"], mesh.shape["gy"]),
        mesh=mesh,
        in_specs=in_specs,
        out_specs=out_specs,
        check_vma=False,
    )
```

```python
import functools

import jax
import jax.numpy as jnp
from jax import lax
from jax.experimental import pallas as pl
from jax.experimental.pallas import tpu as pltpu
from jax.sharding import PartitionSpec as P

NEWTON = 2
SWEEPS = 4
PLANES = 4
PLANE_ORDER = (0, 1, 3, 2)
CHUNK_ORDER = (10, 9, 11, 6, 14, 5, 7, 13, 15, 8, 2, 4, 12, 1, 3, 0)
WELLS_STEP = 16
CHUNK = 4
F32 = jnp.float32
BF16 = jnp.bfloat16
MESH = pl.DeviceIdType.MESH


def halves(x):
    high = x.astype(BF16)
    return high, (x - high.astype(F32)).astype(BF16)


def onehot(size, index):
    rows = lax.broadcasted_iota(jnp.int32, (size, index.shape[1]), 0)
    return jnp.where(rows == index, 1.0, 0.0).astype(BF16)


def kernel(
    n_gx, n_gy, layers, wells,
    state_in, right_in, rock_in, table, cells_in, slots_in, inverse_in,
    state_out, rates_out,
    right, rock, cells, slots, inverse, load_sem,
    coeff, forcing, factor, corr, split, send1, recv1, split2, rows, send2, recv2, total3, total4, decay,
    xs, xr, ys, yr,
    send1_sem, recv1_sem, send2_sem, recv2_sem, rim_send, rim_recv,
):
    gx, gy = lax.axis_index("gx"), lax.axis_index("gy")
    devices = n_gx * n_gy
    me = gx * n_gy + gy
    cell_rows = layers * 8
    tiles = 4 * layers
    group = devices // PLANES
    my_group = lax.div(me, group)

    def place(device):
        return (lax.div(device, n_gy), lax.rem(device, n_gy))

    loads = [
        pltpu.make_async_copy(source, target, load_sem.at[k])
        for k, (source, target) in enumerate(
            (
                (rock_in, rock),
                (state_in, state_out),
                (cells_in, cells),
                (right_in, right),
                (slots_in, slots),
                (inverse_in, inverse),
            )
        )
    ]
    for load in loads:
        load.start()

    xr[...] = jnp.zeros_like(xr)
    yr[...] = jnp.zeros_like(yr)

    barrier = pltpu.get_barrier_semaphore()

    def greet(step, carry):
        pl.semaphore_signal(
            barrier, inc=1, device_id=place(lax.rem(me + step, devices)), device_id_type=MESH
        )
        return carry

    lax.fori_loop(1, devices, greet, 0)

    loads[0].wait()

    def coefficients(i, inner):
        at = pl.ds(pl.multiple_of(i * 8, 8), 8)
        kinds = rock[at, :]
        picked = [kinds == kind for kind in range(8)]
        for c in range(4):
            value = jnp.full((8, 128), 6.0, F32)
            for kind in range(8):
                value = value + jnp.where(picked[kind], table[c, kind], 0.0)
            coeff[pl.ds(pl.multiple_of(c * cell_rows + i * 8, 8), 8), :] = value
        return inner

    lax.fori_loop(0, layers, coefficients, 0, unroll=2)
    first = lax.broadcasted_iota(jnp.int32, decay.shape, 0)
    second = lax.broadcasted_iota(jnp.int32, decay.shape, 1)
    gap = (second - first).astype(F32)
    decay[...] = jnp.where(
        gap >= 0, 0.3 * jnp.exp(jnp.maximum(gap, 0.0) * -0.10536051565782628), 0.0
    )
    for load in loads[1:]:
        load.wait()

    lane = lax.broadcasted_iota(jnp.int32, (8, 128), 1)
    sub = lax.broadcasted_iota(jnp.int32, (8, 128), 0)

    def rim_copies(turn, c):
        right_x = (lax.rem(gx + 1, n_gx), gy)
        left_x = (lax.rem(gx + n_gx - 1, n_gx), gy)
        right_y = (gx, lax.rem(gy + 1, n_gy))
        left_y = (gx, lax.rem(gy + n_gy - 1, n_gy))
        mine = pl.ds(pl.multiple_of(c * layers, layers), layers)
        plan = (
            (xs.at[turn, 1, mine], xr.at[turn, 0, mine], right_x),
            (xs.at[turn, 0, mine], xr.at[turn, 1, mine], left_x),
            (ys.at[turn, c], yr.at[turn, c, 0], right_y),
            (ys.at[turn, c], yr.at[turn, c, 1], left_y),
        )
        return [
            pltpu.make_async_remote_copy(
                src_ref=src,
                dst_ref=dst,
                send_sem=rim_send.at[turn, c, k],
                recv_sem=rim_recv.at[turn, c, k],
                device_id=target,
                device_id_type=MESH,
            )
            for k, (src, dst, target) in enumerate(plan)
        ]

    def tile_of(c, z):
        return pl.ds(pl.multiple_of(c * cell_rows + z * 8, 8), 8)

    def pack(z, value, packed):
        return jnp.where((lane >> 1) == z, pltpu.roll(value, 2 * z + 1, axis=1), packed)

    def send_rims(turn, c, field, packed):
        mine = pl.ds(pl.multiple_of(c * layers, layers), layers)
        x_up, x_down, y_up, y_down = rim_copies(turn, c)
        ys[turn, c] = packed
        start_pair(y_up, y_down, gy, n_gy)
        xs[turn, 0, mine, :] = field[pl.ds(c * cell_rows, layers, stride=8), :]
        xs[turn, 1, mine, :] = field[pl.ds(c * cell_rows + 7, layers, stride=8), :]
        start_pair(x_up, x_down, gx, n_gx)

    def start_pair(up, down, position, count):
        @pl.when(position < count - 1)
        def _():
            up.start()

        @pl.when(position > 0)
        def _():
            down.start()

    def wait_pair(up, down, position, count):
        @pl.when(position < count - 1)
        def _():
            up.wait_send()
            down.wait_recv()

        @pl.when(position > 0)
        def _():
            down.wait_send()
            up.wait_recv()

    def open_rims(turn, c):
        x_up, x_down, y_up, y_down = rim_copies(turn, c)
        wait_pair(x_up, x_down, gx, n_gx)
        wait_pair(y_up, y_down, gy, n_gy)
        return jnp.where((lane & 1) == 0, yr[turn, c, 0], pltpu.roll(yr[turn, c, 1], 126, axis=1))

    def neighbours(turn, field, c, z, columns):
        value = field[tile_of(c, z), :]
        row = c * layers + z
        column = pltpu.roll(columns, 128 - 2 * z, axis=1) if z else columns
        x_low = jnp.broadcast_to(xr[turn, 0, pl.ds(row, 1), :], (8, 128))
        x_high = jnp.broadcast_to(xr[turn, 1, pl.ds(row, 1), :], (8, 128))
        total = jnp.where(sub == 0, x_low, pltpu.roll(value, 1, axis=0))
        total = total + jnp.where(sub == 7, x_high, pltpu.roll(value, 7, axis=0))
        total = total + jnp.where(lane == 0, column, pltpu.roll(value, 1, axis=1))
        total = total + jnp.where(lane == 127, column, pltpu.roll(value, 127, axis=1))
        if z > 0:
            total = total + field[tile_of(c, z - 1), :]
        if z < layers - 1:
            total = total + field[tile_of(c, z + 1), :]
        return value, total

    no_columns = jnp.zeros((8, 128), F32)

    def split_channel(c):
        high, low = halves(state_out[pl.ds(pl.multiple_of(c * cell_rows, cell_rows), cell_rows), :])
        split[c, :, 0:128] = high
        split[c, :, 128:256] = low

    def split_first(c, carry):
        split_channel(c)
        return carry

    lax.fori_loop(0, 4, split_first, 0)

    def block_copy(source, target, source_slot, target_slot, device, send_sem, recv_sem):
        return pltpu.make_async_remote_copy(
            src_ref=source.at[source_slot],
            dst_ref=target.at[target_slot],
            send_sem=send_sem,
            recv_sem=recv_sem,
            device_id=place(device),
            device_id_type=MESH,
        )

    def newton(n, carry):
        turn = n * SWEEPS

        def gather_pair(pair):
            index = jnp.concatenate([cells[pl.ds(2 * pair + k, 1), :] for k in range(2)], axis=1)
            pick = onehot(128, index & 127)
            pick = jnp.concatenate([pick, pick], axis=0)
            wanted = lax.broadcasted_iota(jnp.int32, (cell_rows, 256), 0) == (index >> 7)
            found = []
            for c in range(4):
                value = jnp.dot(split[c], pick, preferred_element_type=F32)
                found.append(jnp.sum(jnp.where(wanted, value, 0.0), axis=0, keepdims=True))
            found = jnp.concatenate(found, axis=0)
            return found[:, :128], found[:, 128:]


        my_pair = lax.div(me, 2)
        pairs = devices // 2

        def pair_of(chunk, k):
            away = 0
            for i, code in enumerate(CHUNK_ORDER):
                away = jnp.where(chunk == i, code, away)
            chip_x = lax.rem(lax.div(gx, 2) + lax.div(away, 4), 4)
            core = lax.rem(gx + 1 - k // 2, 2)
            chip_z = lax.rem(lax.div(gy, 4) + lax.rem(away, 4), 4)
            half_y = lax.rem(lax.div(gy, 2) + 1 - k % 2, 2)
            return (2 * chip_x + core) * (n_gy // 2) + chip_z * 2 + half_y

        def gather_chunk(chunk):
            for k in range(CHUNK):
                pair = pair_of(chunk, k)
                for side, block in enumerate(gather_pair(pair)):
                    send1[n, 2 * pair + side] = block

        def send_block(target):
            block_copy(send1.at[n], recv1.at[n], target, me, target, send1_sem.at[n], recv1_sem.at[n]).start()

        def send_chunk(chunk, count=CHUNK):
            for k in range(count):
                for side in range(2):
                    send_block(2 * pair_of(chunk, k) + side)

        chunks = pairs // CHUNK
        early = chunks // 2

        def early_step(chunk, inner):
            gather_chunk(chunk)
            return inner

        lax.fori_loop(0, early, early_step, 0)

        @pl.when(n == 0)
        def _():
            pl.semaphore_wait(barrier, devices - 1)

            def first_rims(c, inner):
                packed = no_columns
                for z in range(layers):
                    packed = pack(z, state_out[tile_of(c, z), :], packed)
                send_rims(turn, c, state_out, packed)
                return inner

            lax.fori_loop(0, 4, first_rims, 0)

        def late_step(step, inner):
            send_chunk(2 * step)
            send_chunk(2 * step + 1)
            gather_chunk(early + step)
            return inner

        lax.fori_loop(0, chunks - early - 1, late_step, 0)
        send_chunk(chunks - 2)
        gather_chunk(chunks - 1)
        send_chunk(chunks - 1, CHUNK - 1)
        send_block(4 * my_pair + 1 - me)
        recv1[n, me] = send1[n, me]

        def base(c, inner):
            columns = open_rims(turn, c)
            for z in range(layers):
                at = tile_of(c, z)
                value, near = neighbours(turn, state_out, c, z, columns)
                square = value * value
                forcing[at, :] = coeff[at, :] * value - near + 0.1 * square * value - right[at, :]
                factor[at, :] = 1.0 / (coeff[at, :] + 0.3 * square)
            return inner

        lax.fori_loop(0, 4, base, 0)

        all_blocks = pl.ds(0, devices - 1)
        arrived = pltpu.make_async_remote_copy(
            src_ref=send1.at[n, all_blocks],
            dst_ref=recv1.at[n, all_blocks],
            send_sem=send1_sem.at[n],
            recv_sem=recv1_sem.at[n],
            device_id=place(me),
            device_id_type=MESH,
        )
        arrived.wait_recv()

        high, low = halves(recv1[n].reshape(4 * devices, 128))
        split2[:, 0:128] = high
        split2[:, 128:256] = low
        quarter = lax.broadcasted_iota(jnp.int32, (4 * devices, 256), 0) >> 2

        def owner_gather(w, inner):
            index = slots[pl.ds(w, 1), :]
            pick = onehot(128, index & 127)
            pick = jnp.concatenate([pick, pick], axis=0)
            value = jnp.dot(split2[...], pick, preferred_element_type=F32)
            value = jnp.where(quarter == (index >> 7), value, 0.0)
            value = jnp.sum(value.reshape(devices // 2, 8, 256), axis=0)
            value = value[0:4] + value[4:8]
            rows[0, pl.ds(w, 4, stride=wells), :] = value[:, :128]
            rows[1, pl.ds(w, 4, stride=wells), :] = value[:, 128:]
            return inner

        lax.fori_loop(0, wells, owner_gather, 0, unroll=4)
        flows = []
        for i in range(4):
            sides = []
            for half in range(2):
                at = slice(half * 128, half * 128 + 128)
                flow = inverse[i, 0, :, at] * rows[half, 0:wells, :]
                for j in range(1, 4):
                    flow = flow + inverse[i, j, :, at] * rows[half, j * wells : (j + 1) * wells, :]
                sides.append(flow)
            flows.append(jnp.concatenate(sides, axis=1))
        rates = jnp.dot(
            jnp.concatenate(flows, axis=0),
            decay[...],
            precision=lax.Precision.HIGHEST,
            preferred_element_type=F32,
        )
        rates_out[...] = rates
        rows[0] = rates[:, :128]
        rows[1] = rates[:, 128:]

        def plane_start(away):
            return lax.rem(my_group + away, PLANES) * group

        def owner_scatter(step):
            first_well = step * WELLS_STEP
            width = WELLS_STEP * 256
            index = jnp.concatenate([slots[pl.ds(first_well + k, 1), :] for k in range(WELLS_STEP)], axis=1)
            rate = jnp.concatenate(
                [rows[half, pl.ds(first_well + k, 4, stride=wells), :] for k in range(WELLS_STEP) for half in range(2)],
                axis=1,
            )
            pick = onehot(256, index & 255)
            wanted = (lax.broadcasted_iota(jnp.int32, (2 * devices, width), 0) >> 2) == (index >> 8)
            parts = []
            for half in halves(jnp.concatenate([rate, rate], axis=0)):
                spread = jnp.broadcast_to(half.astype(F32)[None], (devices // 4, 8, width))
                parts.append(jnp.where(wanted, spread.reshape(2 * devices, width), 0.0).astype(BF16))
            return lax.dot_general(
                jnp.concatenate(parts, axis=1),
                jnp.concatenate([pick, pick], axis=1),
                (((1,), (1,)), ((), ())),
                preferred_element_type=F32,
            )

        total3[...] = owner_scatter(0)
        for step in range(1, wells // WELLS_STEP):
            total3[...] += owner_scatter(step)
        for k in range(2):
            send2[n, pairs * k : pairs * (k + 1)] = total3[:, 128 * k : 128 * (k + 1)].reshape(pairs, 4, 128)

        def send_slot(device):
            return lax.rem(device, 2) * pairs + lax.div(device, 2)

        for j in range(PLANES):
            start = plane_start(PLANE_ORDER[j])

            def return_step(step, inner):
                target = start + lax.rem(me + step, group)
                block_copy(
                    send2.at[n], recv2.at[n], send_slot(target), me, target, send2_sem.at[n], recv2_sem.at[n, j]
                ).start()
                return inner

            lax.fori_loop(1 if j == 0 else 0, group, return_step, 0)
        recv2[n, me] = send2[n, send_slot(me)]
        arrived.wait_send()


        def wait_group(j, count):
            some = pl.ds(0, count)
            pltpu.make_async_remote_copy(
                src_ref=send2.at[n, some],
                dst_ref=recv2.at[n, some],
                send_sem=send2_sem.at[n],
                recv_sem=recv2_sem.at[n, j],
                device_id=place(me),
                device_id_type=MESH,
            ).wait_recv()

        for j in range(PLANES):
            wait_group(j, group - 1 if j == 0 else group)
            start = lax.rem(my_group + PLANES - PLANE_ORDER[j], PLANES) * group
            index = jnp.concatenate([cells[pl.ds(start + k, 1), :] for k in range(group)], axis=1)
            value = jnp.concatenate([recv2[n, start + k] for k in range(group)], axis=1)
            lanes = onehot(128, index & 127)
            pick = onehot(cell_rows, index >> 7)
            pick = jnp.concatenate([pick, pick], axis=1)
            high, low = halves(value)
            spread = jnp.concatenate(
                [
                    jnp.concatenate([lanes * high[c : c + 1], lanes * low[c : c + 1]], axis=1)
                    for c in range(4)
                ],
                axis=0,
            )
            found = lax.dot_general(pick, spread, (((1,), (1,)), ((), ())), preferred_element_type=F32)
            if j == 0:
                total4[...] = found
            else:
                total4[...] += found
        sent = pl.ds(0, devices - 1)
        pltpu.make_async_remote_copy(
            src_ref=send2.at[n, sent],
            dst_ref=recv2.at[n, sent],
            send_sem=send2_sem.at[n],
            recv_sem=recv2_sem.at[n, 0],
            device_id=place(me),
            device_id_type=MESH,
        ).wait_send()

        def first_sweep(c, inner):
            packed = no_columns
            for z in range(layers):
                at = tile_of(c, z)
                inflow = total4[z * 8 : z * 8 + 8, pl.ds(pl.multiple_of(c * 128, 128), 128)]
                value = forcing[at, :] - inflow
                forcing[at, :] = value
                value = value * factor[at, :]
                corr[0, at, :] = value
                packed = pack(z, value, packed)
            send_rims(turn + 1, c, corr.at[0], packed)
            return inner

        lax.fori_loop(0, 4, first_sweep, 0)
        for k in range(1, SWEEPS):
            now, later = corr.at[(k - 1) % 2], corr.at[k % 2]

            def sweep(c, inner):
                columns = open_rims(turn + k, c)
                packed = no_columns
                for z in range(layers):
                    at = tile_of(c, z)
                    _, near = neighbours(turn + k, now, c, z, columns)
                    value = (forcing[at, :] + near) * factor[at, :]
                    if k < SWEEPS - 1:
                        later[at, :] = value
                    else:
                        value = state_out[at, :] - value
                        state_out[at, :] = value
                    packed = pack(z, value, packed)
                if k < SWEEPS - 1:
                    send_rims(turn + k + 1, c, later, packed)
                else:

                    @pl.when(n < NEWTON - 1)
                    def _():
                        send_rims(turn + SWEEPS, c, state_out, packed)
                        split_channel(c)

                return inner

            lax.fori_loop(0, 4, sweep, 0)
        return carry

    lax.fori_loop(0, NEWTON, newton, 0)


def on_device(n_gx, n_gy, state_init, right_side, rock_type, trans_table, perf_cells, seg_slot, seg_inverse):
    channels, layers, rows, columns = state_init.shape
    devices = n_gx * n_gy
    wells, segments = seg_slot.shape
    cell_rows = layers * rows
    tiles = channels * layers
    field = (channels * cell_rows, columns)
    vmem = pl.BlockSpec(memory_space=pltpu.VMEM)
    hbm = pl.BlockSpec(memory_space=pl.ANY)
    smem = pl.BlockSpec(memory_space=pltpu.SMEM)
    turns = NEWTON * SWEEPS
    dma = pltpu.SemaphoreType.DMA
    state, rates = pl.pallas_call(
        functools.partial(kernel, n_gx, n_gy, layers, wells),
        out_shape=(
            jax.ShapeDtypeStruct(field, F32),
            jax.ShapeDtypeStruct((channels * wells, segments), F32),
        ),
        in_specs=[hbm, hbm, hbm, smem, hbm, hbm, hbm],
        out_specs=(vmem, vmem),
        scratch_shapes=[
            pltpu.VMEM(field, F32),
            pltpu.VMEM((cell_rows, columns), jnp.int32),
            pltpu.VMEM((devices, perf_cells.shape[2]), jnp.int32),
            pltpu.VMEM((wells, segments), jnp.int32),
            pltpu.VMEM(seg_inverse.shape, F32),
            dma((6,)),
            pltpu.VMEM(field, F32),
            pltpu.VMEM(field, F32),
            pltpu.VMEM(field, F32),
            pltpu.VMEM((2,) + field, F32),
            pltpu.VMEM((channels, cell_rows, 256), BF16),
            pltpu.VMEM((NEWTON, devices, channels, 128), F32),
            pltpu.VMEM((NEWTON, devices, channels, 128), F32),
            pltpu.VMEM((channels * devices, 256), BF16),
            pltpu.VMEM((2, channels * wells, 128), F32),
            pltpu.VMEM((NEWTON, devices, channels, 128), F32),
            pltpu.VMEM((NEWTON, devices, channels, 128), F32),
            pltpu.VMEM((channels * devices // 2, 256), F32),
            pltpu.VMEM((cell_rows, channels * 128), F32),
            pltpu.VMEM((segments, segments), F32),
            pltpu.VMEM((turns, 2, tiles, 128), F32),
            pltpu.VMEM((turns, 2, tiles, 128), F32),
            pltpu.VMEM((turns, channels, 8, 128), F32),
            pltpu.VMEM((turns, channels, 2, 8, 128), F32),
            dma((NEWTON,)),
            dma((NEWTON,)),
            dma((NEWTON,)),
            dma((NEWTON, PLANES)),
            dma((turns, channels, 4)),
            dma((turns, channels, 4)),
        ],
        compiler_params=pltpu.CompilerParams(
            collective_id=0, has_side_effects=True, vmem_limit_bytes=62 * 1024 * 1024
        ),
        name="newton",
    )(
        state_init.reshape(field),
        right_side.reshape(field),
        rock_type.reshape(cell_rows, columns),
        trans_table,
        perf_cells.reshape(devices, perf_cells.shape[2]),
        seg_slot,
        seg_inverse,
    )
    return state.reshape(state_init.shape), rates.reshape(channels, wells, segments)


def solution(mesh):
    in_specs = (
        P(None, None, "gx", "gy"),
        P(None, None, "gx", "gy"),
        P(None, "gx", "gy"),
        P(),
        P(("gx", "gy"), None, None),
        P(("gx", "gy"), None),
        P(None, None, ("gx", "gy"), None),
    )
    out_specs = (P(None, None, "gx", "gy"), P(None, ("gx", "gy"), None))
    return jax.shard_map(
        functools.partial(on_device, mesh.shape["gx"], mesh.shape["gy"]),
        mesh=mesh,
        in_specs=in_specs,
        out_specs=out_specs,
        check_vma=False,
    )
```

```python
import functools

import jax
import jax.numpy as jnp
from jax import lax
from jax.experimental import pallas as pl
from jax.experimental.pallas import tpu as pltpu
from jax.sharding import PartitionSpec as P

NEWTON = 2
SWEEPS = 4
PLANES = 4
PLANE_ORDER = (0, 1, 3, 2)
CHUNK_ORDER = (10, 9, 11, 6, 14, 5, 7, 13, 15, 8, 2, 4, 12, 1, 3, 0)
WELLS_STEP = 16
CHUNK = 4
F32 = jnp.float32
BF16 = jnp.bfloat16
MESH = pl.DeviceIdType.MESH


def halves(x):
    high = x.astype(BF16)
    return high, (x - high.astype(F32)).astype(BF16)


def onehot(size, index):
    rows = lax.broadcasted_iota(jnp.int32, (size, index.shape[1]), 0)
    return jnp.where(rows == index, 1.0, 0.0).astype(BF16)


def kernel(
    n_gx, n_gy, layers, wells,
    state_in, right_in, rock_in, table, cells_in, slots_in, inverse_in,
    state_out, rates_out,
    right, rock, cells, slots, inverse, load_sem,
    coeff, forcing, factor, corr, split, send1, recv1, split2, rows, send2, recv2, total3, total4, decay, lane_hot, row_hot,
    xs, xr, ys, yr,
    send1_sem, recv1_sem, send2_sem, recv2_sem, rim_send, rim_recv,
):
    gx, gy = lax.axis_index("gx"), lax.axis_index("gy")
    devices = n_gx * n_gy
    me = gx * n_gy + gy
    cell_rows = layers * 8
    tiles = 4 * layers
    group = devices // PLANES
    my_group = lax.div(me, group)

    def place(device):
        return (lax.div(device, n_gy), lax.rem(device, n_gy))

    loads = [
        pltpu.make_async_copy(source, target, load_sem.at[k])
        for k, (source, target) in enumerate(
            (
                (state_in, state_out),
                (cells_in, cells),
                (rock_in, rock),
                (right_in, right),
                (slots_in, slots),
                (inverse_in, inverse),
            )
        )
    ]
    for load in loads:
        load.start()

    xr[...] = jnp.zeros_like(xr)
    yr[...] = jnp.zeros_like(yr)

    barrier = pltpu.get_barrier_semaphore()

    def greet(step, carry):
        pl.semaphore_signal(
            barrier, inc=1, device_id=place(lax.rem(me + step, devices)), device_id_type=MESH
        )
        return carry

    lax.fori_loop(1, devices, greet, 0)

    for load in loads[:2]:
        load.wait()

    lane = lax.broadcasted_iota(jnp.int32, (8, 128), 1)
    sub = lax.broadcasted_iota(jnp.int32, (8, 128), 0)

    def rim_copies(turn, c):
        right_x = (lax.rem(gx + 1, n_gx), gy)
        left_x = (lax.rem(gx + n_gx - 1, n_gx), gy)
        right_y = (gx, lax.rem(gy + 1, n_gy))
        left_y = (gx, lax.rem(gy + n_gy - 1, n_gy))
        mine = pl.ds(pl.multiple_of(c * layers, layers), layers)
        plan = (
            (xs.at[turn, 1, mine], xr.at[turn, 0, mine], right_x),
            (xs.at[turn, 0, mine], xr.at[turn, 1, mine], left_x),
            (ys.at[turn, c], yr.at[turn, c, 0], right_y),
            (ys.at[turn, c], yr.at[turn, c, 1], left_y),
        )
        return [
            pltpu.make_async_remote_copy(
                src_ref=src,
                dst_ref=dst,
                send_sem=rim_send.at[turn, c, k],
                recv_sem=rim_recv.at[turn, c, k],
                device_id=target,
                device_id_type=MESH,
            )
            for k, (src, dst, target) in enumerate(plan)
        ]

    def tile_of(c, z):
        return pl.ds(pl.multiple_of(c * cell_rows + z * 8, 8), 8)

    def pack(z, value, packed):
        return jnp.where((lane >> 1) == z, pltpu.roll(value, 2 * z + 1, axis=1), packed)

    def send_rims(turn, c, field, packed):
        mine = pl.ds(pl.multiple_of(c * layers, layers), layers)
        x_up, x_down, y_up, y_down = rim_copies(turn, c)
        ys[turn, c] = packed
        start_pair(y_up, y_down, gy, n_gy)
        xs[turn, 0, mine, :] = field[pl.ds(c * cell_rows, layers, stride=8), :]
        xs[turn, 1, mine, :] = field[pl.ds(c * cell_rows + 7, layers, stride=8), :]
        start_pair(x_up, x_down, gx, n_gx)

    def start_pair(up, down, position, count):
        @pl.when(position < count - 1)
        def _():
            up.start()

        @pl.when(position > 0)
        def _():
            down.start()

    def wait_pair(up, down, position, count):
        @pl.when(position < count - 1)
        def _():
            up.wait_send()
            down.wait_recv()

        @pl.when(position > 0)
        def _():
            down.wait_send()
            up.wait_recv()

    def open_rims(turn, c):
        x_up, x_down, y_up, y_down = rim_copies(turn, c)
        wait_pair(x_up, x_down, gx, n_gx)
        wait_pair(y_up, y_down, gy, n_gy)
        return jnp.where((lane & 1) == 0, yr[turn, c, 0], pltpu.roll(yr[turn, c, 1], 126, axis=1))

    def neighbours(turn, field, c, z, columns):
        value = field[tile_of(c, z), :]
        row = c * layers + z
        column = pltpu.roll(columns, 128 - 2 * z, axis=1) if z else columns
        x_low = jnp.broadcast_to(xr[turn, 0, pl.ds(row, 1), :], (8, 128))
        x_high = jnp.broadcast_to(xr[turn, 1, pl.ds(row, 1), :], (8, 128))
        total = jnp.where(sub == 0, x_low, pltpu.roll(value, 1, axis=0))
        total = total + jnp.where(sub == 7, x_high, pltpu.roll(value, 7, axis=0))
        total = total + jnp.where(lane == 0, column, pltpu.roll(value, 1, axis=1))
        total = total + jnp.where(lane == 127, column, pltpu.roll(value, 127, axis=1))
        if z > 0:
            total = total + field[tile_of(c, z - 1), :]
        if z < layers - 1:
            total = total + field[tile_of(c, z + 1), :]
        return value, total

    no_columns = jnp.zeros((8, 128), F32)

    def split_channel(c):
        high, low = halves(state_out[pl.ds(pl.multiple_of(c * cell_rows, cell_rows), cell_rows), :])
        split[c, :, 0:128] = high
        split[c, :, 128:256] = low

    def split_first(c, carry):
        split_channel(c)
        return carry

    lax.fori_loop(0, 4, split_first, 0)

    def block_copy(source, target, source_slot, target_slot, device, send_sem, recv_sem):
        return pltpu.make_async_remote_copy(
            src_ref=source.at[source_slot],
            dst_ref=target.at[target_slot],
            send_sem=send_sem,
            recv_sem=recv_sem,
            device_id=place(device),
            device_id_type=MESH,
        )

    def newton(n, carry):
        turn = n * SWEEPS

        def gather_pair(pair):
            index = jnp.concatenate([cells[pl.ds(2 * pair + k, 1), :] for k in range(2)], axis=1)
            pick = onehot(128, index & 127)
            pick = jnp.concatenate([pick, pick], axis=0)
            wanted = lax.broadcasted_iota(jnp.int32, (cell_rows, 256), 0) == (index >> 7)
            found = []
            for c in range(4):
                value = jnp.dot(split[c], pick, preferred_element_type=F32)
                found.append(jnp.sum(jnp.where(wanted, value, 0.0), axis=0, keepdims=True))
            found = jnp.concatenate(found, axis=0)
            return found[:, :128], found[:, 128:]


        my_pair = lax.div(me, 2)
        pairs = devices // 2

        def pair_of(chunk, k):
            away = 0
            for i, code in enumerate(CHUNK_ORDER):
                away = jnp.where(chunk == i, code, away)
            chip_x = lax.rem(lax.div(gx, 2) + lax.div(away, 4), 4)
            core = lax.rem(gx + 1 - k // 2, 2)
            chip_z = lax.rem(lax.div(gy, 4) + lax.rem(away, 4), 4)
            half_y = lax.rem(lax.div(gy, 2) + 1 - k % 2, 2)
            return (2 * chip_x + core) * (n_gy // 2) + chip_z * 2 + half_y

        def gather_chunk(chunk):
            for k in range(CHUNK):
                pair = pair_of(chunk, k)
                for side, block in enumerate(gather_pair(pair)):
                    send1[n, 2 * pair + side] = block

        def send_block(target):
            block_copy(send1.at[n], recv1.at[n], target, me, target, send1_sem.at[n], recv1_sem.at[n]).start()

        def send_chunk(chunk, count=CHUNK):
            for k in range(count):
                for side in range(2):
                    send_block(2 * pair_of(chunk, k) + side)

        chunks = pairs // CHUNK
        early = chunks // 2

        def gather_step(chunk, inner):
            @pl.when((chunk == early) & (n == 0))
            def _():
                pl.semaphore_wait(barrier, devices - 1)

                def first_rims(c, rest):
                    packed = no_columns
                    for z in range(layers):
                        packed = pack(z, state_out[tile_of(c, z), :], packed)
                    send_rims(turn, c, state_out, packed)
                    return rest

                lax.fori_loop(0, 4, first_rims, 0)

            @pl.when(chunk >= early)
            def _():
                send_chunk(2 * (chunk - early))

            @pl.when((chunk >= early) & (chunk < chunks - 1))
            def _():
                send_chunk(2 * (chunk - early) + 1)

            gather_chunk(chunk)
            return inner

        lax.fori_loop(0, chunks, gather_step, 0)
        send_chunk(chunks - 1, CHUNK - 1)
        send_block(4 * my_pair + 1 - me)
        recv1[n, me] = send1[n, me]

        @pl.when(n == 0)
        def _():
            for load in loads[2:]:
                load.wait()

            def coefficients(i, inner):
                at = pl.ds(pl.multiple_of(i * 8, 8), 8)
                kinds = rock[at, :]
                picked = [kinds == kind for kind in range(8)]
                for c in range(4):
                    value = jnp.full((8, 128), 6.0, F32)
                    for kind in range(8):
                        value = value + jnp.where(picked[kind], table[c, kind], 0.0)
                    coeff[pl.ds(pl.multiple_of(c * cell_rows + i * 8, 8), 8), :] = value
                return inner

            lax.fori_loop(0, layers, coefficients, 0, unroll=2)
            first = lax.broadcasted_iota(jnp.int32, decay.shape, 0)
            second = lax.broadcasted_iota(jnp.int32, decay.shape, 1)
            gap = (second - first).astype(F32)
            decay[...] = jnp.where(
                gap >= 0, 0.3 * jnp.exp(jnp.maximum(gap, 0.0) * -0.10536051565782628), 0.0
            )

        def base(c, inner):
            columns = open_rims(turn, c)
            for z in range(layers):
                at = tile_of(c, z)
                value, near = neighbours(turn, state_out, c, z, columns)
                square = value * value
                forcing[at, :] = coeff[at, :] * value - near + 0.1 * square * value - right[at, :]
                factor[at, :] = 1.0 / (coeff[at, :] + 0.3 * square)
            return inner

        lax.fori_loop(0, 4, base, 0)

        all_blocks = pl.ds(0, devices - 1)
        arrived = pltpu.make_async_remote_copy(
            src_ref=send1.at[n, all_blocks],
            dst_ref=recv1.at[n, all_blocks],
            send_sem=send1_sem.at[n],
            recv_sem=recv1_sem.at[n],
            device_id=place(me),
            device_id_type=MESH,
        )
        arrived.wait_recv()

        high, low = halves(recv1[n].reshape(4 * devices, 128))
        split2[:, 0:128] = high
        split2[:, 128:256] = low
        quarter = lax.broadcasted_iota(jnp.int32, (4 * devices, 256), 0) >> 2

        def owner_gather(w, inner):
            index = slots[pl.ds(w, 1), :]
            pick = onehot(128, index & 127)
            pick = jnp.concatenate([pick, pick], axis=0)
            value = jnp.dot(split2[...], pick, preferred_element_type=F32)
            value = jnp.where(quarter == (index >> 7), value, 0.0)
            value = jnp.sum(value.reshape(devices // 2, 8, 256), axis=0)
            value = value[0:4] + value[4:8]
            rows[0, pl.ds(w, 4, stride=wells), :] = value[:, :128]
            rows[1, pl.ds(w, 4, stride=wells), :] = value[:, 128:]
            return inner

        lax.fori_loop(0, wells, owner_gather, 0, unroll=4)
        flows = []
        for i in range(4):
            sides = []
            for half in range(2):
                at = slice(half * 128, half * 128 + 128)
                flow = inverse[i, 0, :, at] * rows[half, 0:wells, :]
                for j in range(1, 4):
                    flow = flow + inverse[i, j, :, at] * rows[half, j * wells : (j + 1) * wells, :]
                sides.append(flow)
            flows.append(jnp.concatenate(sides, axis=1))
        rates = jnp.dot(
            jnp.concatenate(flows, axis=0),
            decay[...],
            precision=lax.Precision.HIGHEST,
            preferred_element_type=F32,
        )
        rates_out[...] = rates
        rows[0] = rates[:, :128]
        rows[1] = rates[:, 128:]

        def plane_start(away):
            return lax.rem(my_group + away, PLANES) * group

        def owner_scatter(step):
            first_well = step * WELLS_STEP
            width = WELLS_STEP * 256
            index = jnp.concatenate([slots[pl.ds(first_well + k, 1), :] for k in range(WELLS_STEP)], axis=1)
            rate = jnp.concatenate(
                [rows[half, pl.ds(first_well + k, 4, stride=wells), :] for k in range(WELLS_STEP) for half in range(2)],
                axis=1,
            )
            pick = onehot(256, index & 255)
            wanted = (lax.broadcasted_iota(jnp.int32, (2 * devices, width), 0) >> 2) == (index >> 8)
            parts = []
            for half in halves(jnp.concatenate([rate, rate], axis=0)):
                spread = jnp.broadcast_to(half.astype(F32)[None], (devices // 4, 8, width))
                parts.append(jnp.where(wanted, spread.reshape(2 * devices, width), 0.0).astype(BF16))
            return lax.dot_general(
                jnp.concatenate(parts, axis=1),
                jnp.concatenate([pick, pick], axis=1),
                (((1,), (1,)), ((), ())),
                preferred_element_type=F32,
            )

        def owner_step(step, inner):
            total3[...] += owner_scatter(step)
            return inner

        total3[...] = jnp.zeros_like(total3)
        lax.fori_loop(0, wells // WELLS_STEP, owner_step, 0)
        for k in range(2):
            send2[n, pairs * k : pairs * (k + 1)] = total3[:, 128 * k : 128 * (k + 1)].reshape(pairs, 4, 128)

        def send_slot(device):
            return lax.rem(device, 2) * pairs + lax.div(device, 2)

        def plane_away(j):
            away = 0
            for i, plane in enumerate(PLANE_ORDER):
                away = jnp.where(j == i, plane, away)
            return away

        def return_plane(j, carry):
            start = plane_start(plane_away(j))

            def return_step(step, inner):
                target = start + lax.rem(me + step, group)
                block_copy(
                    send2.at[n], recv2.at[n], send_slot(target), me, target, send2_sem.at[n], recv2_sem.at[n, j]
                ).start()
                return inner

            @pl.when(j > 0)
            def _():
                return_step(0, 0)

            lax.fori_loop(1, group, return_step, 0, unroll=True)
            return carry

        lax.fori_loop(0, PLANES, return_plane, 0)
        recv2[n, me] = send2[n, send_slot(me)]
        arrived.wait_send()


        def wait_group(j, count):
            some = pl.ds(0, count)
            pltpu.make_async_remote_copy(
                src_ref=send2.at[n, some],
                dst_ref=recv2.at[n, some],
                send_sem=send2_sem.at[n],
                recv_sem=recv2_sem.at[n, j],
                device_id=place(me),
                device_id_type=MESH,
            ).wait_recv()

        def owners_of(j):
            return lax.rem(my_group + PLANES - plane_away(j), PLANES) * group

        def cells_of(j, inner):
            start = owners_of(j)
            index = jnp.concatenate([cells[pl.ds(start + k, 1), :] for k in range(group)], axis=1)
            lane_hot[j] = onehot(128, index & 127)
            row_hot[j] = onehot(cell_rows, index >> 7)
            return inner

        @pl.when(n == 0)
        def _():
            lax.fori_loop(0, PLANES, cells_of, 0)

        def inflow_plane(j, inner):
            @pl.when(j == 0)
            def _():
                wait_group(j, group - 1)

            @pl.when(j > 0)
            def _():
                wait_group(j, group)

            start = owners_of(j)
            value = jnp.concatenate([recv2[n, start + k] for k in range(group)], axis=1)
            lanes = lane_hot[j]
            pick = row_hot[j]
            pick = jnp.concatenate([pick, pick], axis=1)
            high, low = halves(value)
            spread = jnp.concatenate(
                [
                    jnp.concatenate([lanes * high[c : c + 1], lanes * low[c : c + 1]], axis=1)
                    for c in range(4)
                ],
                axis=0,
            )
            total4[...] += lax.dot_general(pick, spread, (((1,), (1,)), ((), ())), preferred_element_type=F32)
            return inner

        total4[...] = jnp.zeros_like(total4)
        lax.fori_loop(0, PLANES, inflow_plane, 0)
        sent = pl.ds(0, devices - 1)
        pltpu.make_async_remote_copy(
            src_ref=send2.at[n, sent],
            dst_ref=recv2.at[n, sent],
            send_sem=send2_sem.at[n],
            recv_sem=recv2_sem.at[n, 0],
            device_id=place(me),
            device_id_type=MESH,
        ).wait_send()

        def first_sweep(c, inner):
            packed = no_columns
            for z in range(layers):
                at = tile_of(c, z)
                inflow = total4[z * 8 : z * 8 + 8, pl.ds(pl.multiple_of(c * 128, 128), 128)]
                value = forcing[at, :] - inflow
                forcing[at, :] = value
                value = value * factor[at, :]
                corr[0, at, :] = value
                packed = pack(z, value, packed)
            send_rims(turn + 1, c, corr.at[0], packed)
            return inner

        lax.fori_loop(0, 4, first_sweep, 0)
        for k in range(1, SWEEPS):
            now, later = corr.at[(k - 1) % 2], corr.at[k % 2]

            def sweep(c, inner):
                columns = open_rims(turn + k, c)
                packed = no_columns
                for z in range(layers):
                    at = tile_of(c, z)
                    _, near = neighbours(turn + k, now, c, z, columns)
                    value = (forcing[at, :] + near) * factor[at, :]
                    if k < SWEEPS - 1:
                        later[at, :] = value
                    else:
                        value = state_out[at, :] - value
                        state_out[at, :] = value
                    packed = pack(z, value, packed)
                if k < SWEEPS - 1:
                    send_rims(turn + k + 1, c, later, packed)
                else:

                    @pl.when(n < NEWTON - 1)
                    def _():
                        send_rims(turn + SWEEPS, c, state_out, packed)
                        split_channel(c)

                return inner

            lax.fori_loop(0, 4, sweep, 0)
        return carry

    lax.fori_loop(0, NEWTON, newton, 0)


def on_device(n_gx, n_gy, state_init, right_side, rock_type, trans_table, perf_cells, seg_slot, seg_inverse):
    channels, layers, rows, columns = state_init.shape
    devices = n_gx * n_gy
    wells, segments = seg_slot.shape
    cell_rows = layers * rows
    tiles = channels * layers
    field = (channels * cell_rows, columns)
    vmem = pl.BlockSpec(memory_space=pltpu.VMEM)
    hbm = pl.BlockSpec(memory_space=pl.ANY)
    smem = pl.BlockSpec(memory_space=pltpu.SMEM)
    turns = NEWTON * SWEEPS
    dma = pltpu.SemaphoreType.DMA
    state, rates = pl.pallas_call(
        functools.partial(kernel, n_gx, n_gy, layers, wells),
        out_shape=(
            jax.ShapeDtypeStruct(field, F32),
            jax.ShapeDtypeStruct((channels * wells, segments), F32),
        ),
        in_specs=[hbm, hbm, hbm, smem, hbm, hbm, hbm],
        out_specs=(vmem, vmem),
        scratch_shapes=[
            pltpu.VMEM(field, F32),
            pltpu.VMEM((cell_rows, columns), jnp.int32),
            pltpu.VMEM((devices, perf_cells.shape[2]), jnp.int32),
            pltpu.VMEM((wells, segments), jnp.int32),
            pltpu.VMEM(seg_inverse.shape, F32),
            dma((6,)),
            pltpu.VMEM(field, F32),
            pltpu.VMEM(field, F32),
            pltpu.VMEM(field, F32),
            pltpu.VMEM((2,) + field, F32),
            pltpu.VMEM((channels, cell_rows, 256), BF16),
            pltpu.VMEM((NEWTON, devices, channels, 128), F32),
            pltpu.VMEM((NEWTON, devices, channels, 128), F32),
            pltpu.VMEM((channels * devices, 256), BF16),
            pltpu.VMEM((2, channels * wells, 128), F32),
            pltpu.VMEM((NEWTON, devices, channels, 128), F32),
            pltpu.VMEM((NEWTON, devices, channels, 128), F32),
            pltpu.VMEM((channels * devices // 2, 256), F32),
            pltpu.VMEM((cell_rows, channels * 128), F32),
            pltpu.VMEM((segments, segments), F32),
            pltpu.VMEM((PLANES, 128, devices // PLANES * 128), BF16),
            pltpu.VMEM((PLANES, cell_rows, devices // PLANES * 128), BF16),
            pltpu.VMEM((turns, 2, tiles, 128), F32),
            pltpu.VMEM((turns, 2, tiles, 128), F32),
            pltpu.VMEM((turns, channels, 8, 128), F32),
            pltpu.VMEM((turns, channels, 2, 8, 128), F32),
            dma((NEWTON,)),
            dma((NEWTON,)),
            dma((NEWTON,)),
            dma((NEWTON, PLANES)),
            dma((turns, channels, 4)),
            dma((turns, channels, 4)),
        ],
        compiler_params=pltpu.CompilerParams(
            collective_id=0, has_side_effects=True, vmem_limit_bytes=62 * 1024 * 1024
        ),
        name="newton",
    )(
        state_init.reshape(field),
        right_side.reshape(field),
        rock_type.reshape(cell_rows, columns),
        trans_table,
        perf_cells.reshape(devices, perf_cells.shape[2]),
        seg_slot,
        seg_inverse,
    )
    return state.reshape(state_init.shape), rates.reshape(channels, wells, segments)


def solution(mesh):
    in_specs = (
        P(None, None, "gx", "gy"),
        P(None, None, "gx", "gy"),
        P(None, "gx", "gy"),
        P(),
        P(("gx", "gy"), None, None),
        P(("gx", "gy"), None),
        P(None, None, ("gx", "gy"), None),
    )
    out_specs = (P(None, None, "gx", "gy"), P(None, ("gx", "gy"), None))
    return jax.shard_map(
        functools.partial(on_device, mesh.shape["gx"], mesh.shape["gy"]),
        mesh=mesh,
        in_specs=in_specs,
        out_specs=out_specs,
        check_vma=False,
    )
```

```python
import functools

import jax
import jax.numpy as jnp
from jax import lax
from jax.experimental import pallas as pl
from jax.experimental.pallas import tpu as pltpu
from jax.sharding import PartitionSpec as P

NEWTON = 2
SWEEPS = 4
PLANES = 4
PLANE_ORDER = (0, 1, 3, 2)
CHUNK_ORDER = (10, 9, 11, 6, 14, 5, 7, 13, 15, 8, 2, 4, 12, 1, 3, 0)
WELLS_STEP = 16
CHUNK = 4
F32 = jnp.float32
BF16 = jnp.bfloat16
MESH = pl.DeviceIdType.MESH


def halves(x):
    high = x.astype(BF16)
    return high, (x - high.astype(F32)).astype(BF16)


def onehot(size, index):
    rows = lax.broadcasted_iota(jnp.int32, (size, index.shape[1]), 0)
    return jnp.where(rows == index, 1.0, 0.0).astype(BF16)


def kernel(
    n_gx, n_gy, layers, wells,
    state_in, right_in, rock_in, table, cells_in, slots_in, inverse_in,
    state_out, rates_out,
    right, rock, cells, slots, inverse, load_sem,
    coeff, forcing, factor, corr, split, send1, recv1, split2, rows, send2, recv2, total3, total4, decay, lane_hot, row_hot,
    xs, xr, ys, yr,
    send1_sem, recv1_sem, send2_sem, recv2_sem, rim_send, rim_recv,
):
    gx, gy = lax.axis_index("gx"), lax.axis_index("gy")
    devices = n_gx * n_gy
    me = gx * n_gy + gy
    cell_rows = layers * 8
    tiles = 4 * layers
    group = devices // PLANES
    my_group = lax.div(me, group)

    def place(device):
        return (lax.div(device, n_gy), lax.rem(device, n_gy))

    loads = [
        pltpu.make_async_copy(source, target, load_sem.at[k])
        for k, (source, target) in enumerate(
            (
                (state_in, state_out),
                (cells_in, cells),
                (rock_in, rock),
                (right_in, right),
                (slots_in, slots),
                (inverse_in, inverse),
            )
        )
    ]
    for load in loads:
        load.start()

    xr[...] = jnp.zeros_like(xr)
    yr[...] = jnp.zeros_like(yr)

    barrier = pltpu.get_barrier_semaphore()

    def greet(step, carry):
        pl.semaphore_signal(
            barrier, inc=1, device_id=place(lax.rem(me + step, devices)), device_id_type=MESH
        )
        return carry

    lax.fori_loop(1, devices, greet, 0)

    for load in loads[:2]:
        load.wait()

    lane = lax.broadcasted_iota(jnp.int32, (8, 128), 1)
    sub = lax.broadcasted_iota(jnp.int32, (8, 128), 0)

    def rim_copies(turn, c):
        right_x = (lax.rem(gx + 1, n_gx), gy)
        left_x = (lax.rem(gx + n_gx - 1, n_gx), gy)
        right_y = (gx, lax.rem(gy + 1, n_gy))
        left_y = (gx, lax.rem(gy + n_gy - 1, n_gy))
        mine = pl.ds(pl.multiple_of(c * layers, layers), layers)
        plan = (
            (xs.at[turn, 1, mine], xr.at[turn, 0, mine], right_x),
            (xs.at[turn, 0, mine], xr.at[turn, 1, mine], left_x),
            (ys.at[turn, c], yr.at[turn, c, 0], right_y),
            (ys.at[turn, c], yr.at[turn, c, 1], left_y),
        )
        return [
            pltpu.make_async_remote_copy(
                src_ref=src,
                dst_ref=dst,
                send_sem=rim_send.at[turn, c, k],
                recv_sem=rim_recv.at[turn, c, k],
                device_id=target,
                device_id_type=MESH,
            )
            for k, (src, dst, target) in enumerate(plan)
        ]

    def tile_of(c, z):
        return pl.ds(pl.multiple_of(c * cell_rows + z * 8, 8), 8)

    def pack(z, value, packed):
        return jnp.where((lane >> 1) == z, pltpu.roll(value, 2 * z + 1, axis=1), packed)

    def send_rims(turn, c, field, packed):
        mine = pl.ds(pl.multiple_of(c * layers, layers), layers)
        x_up, x_down, y_up, y_down = rim_copies(turn, c)
        ys[turn, c] = packed
        start_pair(y_up, y_down, gy, n_gy)
        xs[turn, 0, mine, :] = field[pl.ds(c * cell_rows, layers, stride=8), :]
        xs[turn, 1, mine, :] = field[pl.ds(c * cell_rows + 7, layers, stride=8), :]
        start_pair(x_up, x_down, gx, n_gx)

    def start_pair(up, down, position, count):
        @pl.when(position < count - 1)
        def _():
            up.start()

        @pl.when(position > 0)
        def _():
            down.start()

    def wait_pair(up, down, position, count):
        @pl.when(position < count - 1)
        def _():
            up.wait_send()
            down.wait_recv()

        @pl.when(position > 0)
        def _():
            down.wait_send()
            up.wait_recv()

    def open_rims(turn, c):
        x_up, x_down, y_up, y_down = rim_copies(turn, c)
        wait_pair(x_up, x_down, gx, n_gx)
        wait_pair(y_up, y_down, gy, n_gy)
        return jnp.where((lane & 1) == 0, yr[turn, c, 0], pltpu.roll(yr[turn, c, 1], 126, axis=1))

    def neighbours(turn, field, c, z, columns):
        value = field[tile_of(c, z), :]
        row = c * layers + z
        column = pltpu.roll(columns, 128 - 2 * z, axis=1) if z else columns
        x_low = jnp.broadcast_to(xr[turn, 0, pl.ds(row, 1), :], (8, 128))
        x_high = jnp.broadcast_to(xr[turn, 1, pl.ds(row, 1), :], (8, 128))
        total = jnp.where(sub == 0, x_low, pltpu.roll(value, 1, axis=0))
        total = total + jnp.where(sub == 7, x_high, pltpu.roll(value, 7, axis=0))
        total = total + jnp.where(lane == 0, column, pltpu.roll(value, 1, axis=1))
        total = total + jnp.where(lane == 127, column, pltpu.roll(value, 127, axis=1))
        if z > 0:
            total = total + field[tile_of(c, z - 1), :]
        if z < layers - 1:
            total = total + field[tile_of(c, z + 1), :]
        return value, total

    no_columns = jnp.zeros((8, 128), F32)

    def split_channel(c):
        high, low = halves(state_out[pl.ds(pl.multiple_of(c * cell_rows, cell_rows), cell_rows), :])
        split[c, :, 0:128] = high
        split[c, :, 128:256] = low

    def split_first(c, carry):
        split_channel(c)
        return carry

    lax.fori_loop(0, 4, split_first, 0)

    def block_copy(source, target, source_slot, target_slot, device, send_sem, recv_sem):
        return pltpu.make_async_remote_copy(
            src_ref=source.at[source_slot],
            dst_ref=target.at[target_slot],
            send_sem=send_sem,
            recv_sem=recv_sem,
            device_id=place(device),
            device_id_type=MESH,
        )

    def newton(n, carry):
        turn = n * SWEEPS

        def gather_pair(pair):
            index = jnp.concatenate([cells[pl.ds(2 * pair + k, 1), :] for k in range(2)], axis=1)
            pick = onehot(128, index & 127)
            pick = jnp.concatenate([pick, pick], axis=0)
            wanted = lax.broadcasted_iota(jnp.int32, (cell_rows, 256), 0) == (index >> 7)
            found = []
            for c in range(4):
                value = jnp.dot(split[c], pick, preferred_element_type=F32)
                found.append(jnp.sum(jnp.where(wanted, value, 0.0), axis=0, keepdims=True))
            found = jnp.concatenate(found, axis=0)
            return found[:, :128], found[:, 128:]


        my_pair = lax.div(me, 2)
        pairs = devices // 2

        def pair_of(chunk, k):
            away = 0
            for i, code in enumerate(CHUNK_ORDER):
                away = jnp.where(chunk == i, code, away)
            chip_x = lax.rem(lax.div(gx, 2) + lax.div(away, 4), 4)
            core = lax.rem(gx + 1 - k // 2, 2)
            chip_z = lax.rem(lax.div(gy, 4) + lax.rem(away, 4), 4)
            half_y = lax.rem(lax.div(gy, 2) + 1 - k % 2, 2)
            return (2 * chip_x + core) * (n_gy // 2) + chip_z * 2 + half_y

        def gather_chunk(chunk):
            for k in range(CHUNK):
                pair = pair_of(chunk, k)
                for side, block in enumerate(gather_pair(pair)):
                    send1[n, 2 * pair + side] = block

        def send_block(target):
            block_copy(send1.at[n], recv1.at[n], target, me, target, send1_sem.at[n], recv1_sem.at[n]).start()

        def send_chunk(chunk, count=CHUNK):
            for k in range(count):
                for side in range(2):
                    send_block(2 * pair_of(chunk, k) + side)

        chunks = pairs // CHUNK
        early = chunks // 2

        def early_step(chunk, inner):
            gather_chunk(chunk)
            return inner

        lax.fori_loop(0, early, early_step, 0)

        @pl.when(n == 0)
        def _():
            pl.semaphore_wait(barrier, devices - 1)

            def first_rims(c, rest):
                packed = no_columns
                for z in range(layers):
                    packed = pack(z, state_out[tile_of(c, z), :], packed)
                send_rims(turn, c, state_out, packed)
                return rest

            lax.fori_loop(0, 4, first_rims, 0)

        def late_step(step, inner):
            send_chunk(2 * step)
            gather_chunk(early + step)
            send_chunk(2 * step + 1)
            return inner

        lax.fori_loop(0, chunks - early - 1, late_step, 0)
        send_chunk(chunks - 2)
        gather_chunk(chunks - 1)
        send_chunk(chunks - 1, CHUNK - 1)
        send_block(4 * my_pair + 1 - me)
        recv1[n, me] = send1[n, me]

        @pl.when(n == 0)
        def _():
            for load in loads[2:]:
                load.wait()

            def coefficients(i, inner):
                at = pl.ds(pl.multiple_of(i * 8, 8), 8)
                kinds = rock[at, :]
                picked = [kinds == kind for kind in range(8)]
                for c in range(4):
                    value = jnp.full((8, 128), 6.0, F32)
                    for kind in range(8):
                        value = value + jnp.where(picked[kind], table[c, kind], 0.0)
                    coeff[pl.ds(pl.multiple_of(c * cell_rows + i * 8, 8), 8), :] = value
                return inner

            lax.fori_loop(0, layers, coefficients, 0, unroll=2)
            first = lax.broadcasted_iota(jnp.int32, decay.shape, 0)
            second = lax.broadcasted_iota(jnp.int32, decay.shape, 1)
            gap = (second - first).astype(F32)
            decay[...] = jnp.where(
                gap >= 0, 0.3 * jnp.exp(jnp.maximum(gap, 0.0) * -0.10536051565782628), 0.0
            )

        def base(c, inner):
            columns = open_rims(turn, c)
            for z in range(layers):
                at = tile_of(c, z)
                value, near = neighbours(turn, state_out, c, z, columns)
                square = value * value
                forcing[at, :] = coeff[at, :] * value - near + 0.1 * square * value - right[at, :]
                factor[at, :] = 1.0 / (coeff[at, :] + 0.3 * square)
            return inner

        lax.fori_loop(0, 4, base, 0)

        all_blocks = pl.ds(0, devices - 1)
        arrived = pltpu.make_async_remote_copy(
            src_ref=send1.at[n, all_blocks],
            dst_ref=recv1.at[n, all_blocks],
            send_sem=send1_sem.at[n],
            recv_sem=recv1_sem.at[n],
            device_id=place(me),
            device_id_type=MESH,
        )
        arrived.wait_recv()

        high, low = halves(recv1[n].reshape(4 * devices, 128))
        split2[:, 0:128] = high
        split2[:, 128:256] = low
        quarter = lax.broadcasted_iota(jnp.int32, (4 * devices, 256), 0) >> 2

        def owner_gather(w, inner):
            index = slots[pl.ds(w, 1), :]
            pick = onehot(128, index & 127)
            pick = jnp.concatenate([pick, pick], axis=0)
            value = jnp.dot(split2[...], pick, preferred_element_type=F32)
            value = jnp.where(quarter == (index >> 7), value, 0.0)
            value = jnp.sum(value.reshape(devices // 2, 8, 256), axis=0)
            value = value[0:4] + value[4:8]
            rows[0, pl.ds(w, 4, stride=wells), :] = value[:, :128]
            rows[1, pl.ds(w, 4, stride=wells), :] = value[:, 128:]
            return inner

        lax.fori_loop(0, wells, owner_gather, 0, unroll=8)
        flows = []
        for i in range(4):
            sides = []
            for half in range(2):
                at = slice(half * 128, half * 128 + 128)
                flow = inverse[i, 0, :, at] * rows[half, 0:wells, :]
                for j in range(1, 4):
                    flow = flow + inverse[i, j, :, at] * rows[half, j * wells : (j + 1) * wells, :]
                sides.append(flow)
            flows.append(jnp.concatenate(sides, axis=1))
        rates = jnp.dot(
            jnp.concatenate(flows, axis=0),
            decay[...],
            precision=lax.Precision.HIGHEST,
            preferred_element_type=F32,
        )
        rates_out[...] = rates
        rows[0] = rates[:, :128]
        rows[1] = rates[:, 128:]

        def plane_start(away):
            return lax.rem(my_group + away, PLANES) * group

        def owner_scatter(step):
            first_well = step * WELLS_STEP
            width = WELLS_STEP * 256
            index = jnp.concatenate([slots[pl.ds(first_well + k, 1), :] for k in range(WELLS_STEP)], axis=1)
            rate = jnp.concatenate(
                [rows[half, pl.ds(first_well + k, 4, stride=wells), :] for k in range(WELLS_STEP) for half in range(2)],
                axis=1,
            )
            pick = onehot(256, index & 255)
            wanted = (lax.broadcasted_iota(jnp.int32, (2 * devices, width), 0) >> 2) == (index >> 8)
            parts = []
            for half in halves(jnp.concatenate([rate, rate], axis=0)):
                spread = jnp.broadcast_to(half.astype(F32)[None], (devices // 4, 8, width))
                parts.append(jnp.where(wanted, spread.reshape(2 * devices, width), 0.0).astype(BF16))
            return lax.dot_general(
                jnp.concatenate(parts, axis=1),
                jnp.concatenate([pick, pick], axis=1),
                (((1,), (1,)), ((), ())),
                preferred_element_type=F32,
            )

        def owner_step(step, inner):
            total3[...] += owner_scatter(step)
            return inner

        total3[...] = jnp.zeros_like(total3)
        lax.fori_loop(0, wells // WELLS_STEP, owner_step, 0)
        for k in range(2):
            send2[n, pairs * k : pairs * (k + 1)] = total3[:, 128 * k : 128 * (k + 1)].reshape(pairs, 4, 128)

        def send_slot(device):
            return lax.rem(device, 2) * pairs + lax.div(device, 2)

        def plane_away(j):
            away = 0
            for i, plane in enumerate(PLANE_ORDER):
                away = jnp.where(j == i, plane, away)
            return away

        def return_plane(j, carry):
            start = plane_start(plane_away(j))

            def return_step(step, inner):
                target = start + lax.rem(me + step, group)
                block_copy(
                    send2.at[n], recv2.at[n], send_slot(target), me, target, send2_sem.at[n], recv2_sem.at[n, j]
                ).start()
                return inner

            @pl.when(j > 0)
            def _():
                return_step(0, 0)

            lax.fori_loop(1, group, return_step, 0, unroll=True)
            return carry

        lax.fori_loop(0, PLANES, return_plane, 0)
        recv2[n, me] = send2[n, send_slot(me)]
        arrived.wait_send()


        def wait_group(j, count):
            some = pl.ds(0, count)
            pltpu.make_async_remote_copy(
                src_ref=send2.at[n, some],
                dst_ref=recv2.at[n, some],
                send_sem=send2_sem.at[n],
                recv_sem=recv2_sem.at[n, j],
                device_id=place(me),
                device_id_type=MESH,
            ).wait_recv()

        def owners_of(j):
            return lax.rem(my_group + PLANES - plane_away(j), PLANES) * group

        def cells_of(j, inner):
            start = owners_of(j)
            index = jnp.concatenate([cells[pl.ds(start + k, 1), :] for k in range(group)], axis=1)
            lane_hot[j] = onehot(128, index & 127)
            row_hot[j] = onehot(cell_rows, index >> 7)
            return inner

        @pl.when(n == 0)
        def _():
            lax.fori_loop(0, PLANES, cells_of, 0)

        def inflow_plane(j, inner):
            @pl.when(j == 0)
            def _():
                wait_group(j, group - 1)

            @pl.when(j > 0)
            def _():
                wait_group(j, group)

            start = owners_of(j)
            value = jnp.concatenate([recv2[n, start + k] for k in range(group)], axis=1)
            lanes = lane_hot[j]
            pick = row_hot[j]
            pick = jnp.concatenate([pick, pick], axis=1)
            high, low = halves(value)
            spread = jnp.concatenate(
                [
                    jnp.concatenate([lanes * high[c : c + 1], lanes * low[c : c + 1]], axis=1)
                    for c in range(4)
                ],
                axis=0,
            )
            total4[...] += lax.dot_general(pick, spread, (((1,), (1,)), ((), ())), preferred_element_type=F32)
            return inner

        total4[...] = jnp.zeros_like(total4)
        lax.fori_loop(0, PLANES, inflow_plane, 0)
        sent = pl.ds(0, devices - 1)
        pltpu.make_async_remote_copy(
            src_ref=send2.at[n, sent],
            dst_ref=recv2.at[n, sent],
            send_sem=send2_sem.at[n],
            recv_sem=recv2_sem.at[n, 0],
            device_id=place(me),
            device_id_type=MESH,
        ).wait_send()

        def first_sweep(c, inner):
            packed = no_columns
            for z in range(layers):
                at = tile_of(c, z)
                inflow = total4[z * 8 : z * 8 + 8, pl.ds(pl.multiple_of(c * 128, 128), 128)]
                value = forcing[at, :] - inflow
                forcing[at, :] = value
                value = value * factor[at, :]
                corr[0, at, :] = value
                packed = pack(z, value, packed)
            send_rims(turn + 1, c, corr.at[0], packed)
            return inner

        lax.fori_loop(0, 4, first_sweep, 0)
        for k in range(1, SWEEPS):
            now, later = corr.at[(k - 1) % 2], corr.at[k % 2]

            def sweep(c, inner):
                columns = open_rims(turn + k, c)
                packed = no_columns
                for z in range(layers):
                    at = tile_of(c, z)
                    _, near = neighbours(turn + k, now, c, z, columns)
                    value = (forcing[at, :] + near) * factor[at, :]
                    if k < SWEEPS - 1:
                        later[at, :] = value
                    else:
                        value = state_out[at, :] - value
                        state_out[at, :] = value
                    packed = pack(z, value, packed)
                if k < SWEEPS - 1:
                    send_rims(turn + k + 1, c, later, packed)
                else:

                    @pl.when(n < NEWTON - 1)
                    def _():
                        send_rims(turn + SWEEPS, c, state_out, packed)
                        split_channel(c)

                return inner

            lax.fori_loop(0, 4, sweep, 0)
        return carry

    lax.fori_loop(0, NEWTON, newton, 0)


def on_device(n_gx, n_gy, state_init, right_side, rock_type, trans_table, perf_cells, seg_slot, seg_inverse):
    channels, layers, rows, columns = state_init.shape
    devices = n_gx * n_gy
    wells, segments = seg_slot.shape
    cell_rows = layers * rows
    tiles = channels * layers
    field = (channels * cell_rows, columns)
    vmem = pl.BlockSpec(memory_space=pltpu.VMEM)
    hbm = pl.BlockSpec(memory_space=pl.ANY)
    smem = pl.BlockSpec(memory_space=pltpu.SMEM)
    turns = NEWTON * SWEEPS
    dma = pltpu.SemaphoreType.DMA
    state, rates = pl.pallas_call(
        functools.partial(kernel, n_gx, n_gy, layers, wells),
        out_shape=(
            jax.ShapeDtypeStruct(field, F32),
            jax.ShapeDtypeStruct((channels * wells, segments), F32),
        ),
        in_specs=[hbm, hbm, hbm, smem, hbm, hbm, hbm],
        out_specs=(vmem, vmem),
        scratch_shapes=[
            pltpu.VMEM(field, F32),
            pltpu.VMEM((cell_rows, columns), jnp.int32),
            pltpu.VMEM((devices, perf_cells.shape[2]), jnp.int32),
            pltpu.VMEM((wells, segments), jnp.int32),
            pltpu.VMEM(seg_inverse.shape, F32),
            dma((6,)),
            pltpu.VMEM(field, F32),
            pltpu.VMEM(field, F32),
            pltpu.VMEM(field, F32),
            pltpu.VMEM((2,) + field, F32),
            pltpu.VMEM((channels, cell_rows, 256), BF16),
            pltpu.VMEM((NEWTON, devices, channels, 128), F32),
            pltpu.VMEM((NEWTON, devices, channels, 128), F32),
            pltpu.VMEM((channels * devices, 256), BF16),
            pltpu.VMEM((2, channels * wells, 128), F32),
            pltpu.VMEM((NEWTON, devices, channels, 128), F32),
            pltpu.VMEM((NEWTON, devices, channels, 128), F32),
            pltpu.VMEM((channels * devices // 2, 256), F32),
            pltpu.VMEM((cell_rows, channels * 128), F32),
            pltpu.VMEM((segments, segments), F32),
            pltpu.VMEM((PLANES, 128, devices // PLANES * 128), BF16),
            pltpu.VMEM((PLANES, cell_rows, devices // PLANES * 128), BF16),
            pltpu.VMEM((turns, 2, tiles, 128), F32),
            pltpu.VMEM((turns, 2, tiles, 128), F32),
            pltpu.VMEM((turns, channels, 8, 128), F32),
            pltpu.VMEM((turns, channels, 2, 8, 128), F32),
            dma((NEWTON,)),
            dma((NEWTON,)),
            dma((NEWTON,)),
            dma((NEWTON, PLANES)),
            dma((turns, channels, 4)),
            dma((turns, channels, 4)),
        ],
        compiler_params=pltpu.CompilerParams(
            collective_id=0, has_side_effects=True, vmem_limit_bytes=62 * 1024 * 1024
        ),
        name="newton",
    )(
        state_init.reshape(field),
        right_side.reshape(field),
        rock_type.reshape(cell_rows, columns),
        trans_table,
        perf_cells.reshape(devices, perf_cells.shape[2]),
        seg_slot,
        seg_inverse,
    )
    return state.reshape(state_init.shape), rates.reshape(channels, wells, segments)


def solution(mesh):
    in_specs = (
        P(None, None, "gx", "gy"),
        P(None, None, "gx", "gy"),
        P(None, "gx", "gy"),
        P(),
        P(("gx", "gy"), None, None),
        P(("gx", "gy"), None),
        P(None, None, ("gx", "gy"), None),
    )
    out_specs = (P(None, None, "gx", "gy"), P(None, ("gx", "gy"), None))
    return jax.shard_map(
        functools.partial(on_device, mesh.shape["gx"], mesh.shape["gy"]),
        mesh=mesh,
        in_specs=in_specs,
        out_specs=out_specs,
        check_vma=False,
    )
```

```python
import functools

import jax
import jax.numpy as jnp
from jax import lax
from jax.experimental import pallas as pl
from jax.experimental.pallas import tpu as pltpu
from jax.sharding import PartitionSpec as P

NEWTON = 2
SWEEPS = 4
PLANES = 4
PLANE_ORDER = (0, 1, 3, 2)
CHUNK_ORDER = (10, 9, 11, 6, 14, 5, 7, 13, 15, 8, 2, 4, 12, 1, 3, 0)
WELLS_STEP = 16
CHUNK = 4
F32 = jnp.float32
BF16 = jnp.bfloat16
MESH = pl.DeviceIdType.MESH


def halves(x):
    high = x.astype(BF16)
    return high, (x - high.astype(F32)).astype(BF16)


def onehot(size, index):
    rows = lax.broadcasted_iota(jnp.int32, (size, index.shape[1]), 0)
    return jnp.where(rows == index, 1.0, 0.0).astype(BF16)


def kernel(
    n_gx, n_gy, layers, wells,
    state_in, right_in, rock_in, table, cells_in, slots_in, inverse_in,
    state_out, rates_out,
    right, rock, cells, slots, inverse, load_sem,
    coeff, forcing, factor, corr, split, send1, recv1, split2, rows, send2, recv2, total3, total4, decay, lane_hot, row_hot,
    xs, xr, ys, yr,
    send1_sem, recv1_sem, send2_sem, recv2_sem, rim_send, rim_recv,
):
    gx, gy = lax.axis_index("gx"), lax.axis_index("gy")
    devices = n_gx * n_gy
    me = gx * n_gy + gy
    cell_rows = layers * 8
    tiles = 4 * layers
    group = devices // PLANES
    my_group = lax.div(me, group)

    def place(device):
        return (lax.div(device, n_gy), lax.rem(device, n_gy))

    loads = [
        pltpu.make_async_copy(source, target, load_sem.at[k])
        for k, (source, target) in enumerate(
            (
                (state_in, state_out),
                (cells_in, cells),
                (rock_in, rock),
                (right_in, right),
                (slots_in, slots),
                (inverse_in, inverse),
            )
        )
    ]
    for load in loads:
        load.start()

    xr[...] = jnp.zeros_like(xr)
    yr[...] = jnp.zeros_like(yr)

    barrier = pltpu.get_barrier_semaphore()

    def greet(step, carry):
        pl.semaphore_signal(
            barrier, inc=1, device_id=place(lax.rem(me + step, devices)), device_id_type=MESH
        )
        return carry

    lax.fori_loop(1, devices, greet, 0)

    for load in loads[:2]:
        load.wait()

    lane = lax.broadcasted_iota(jnp.int32, (8, 128), 1)
    sub = lax.broadcasted_iota(jnp.int32, (8, 128), 0)

    def rim_copies(turn, c):
        right_x = (lax.rem(gx + 1, n_gx), gy)
        left_x = (lax.rem(gx + n_gx - 1, n_gx), gy)
        right_y = (gx, lax.rem(gy + 1, n_gy))
        left_y = (gx, lax.rem(gy + n_gy - 1, n_gy))
        mine = pl.ds(pl.multiple_of(c * layers, layers), layers)
        plan = (
            (xs.at[turn, 1, mine], xr.at[turn, 0, mine], right_x),
            (xs.at[turn, 0, mine], xr.at[turn, 1, mine], left_x),
            (ys.at[turn, c], yr.at[turn, c, 0], right_y),
            (ys.at[turn, c], yr.at[turn, c, 1], left_y),
        )
        return [
            pltpu.make_async_remote_copy(
                src_ref=src,
                dst_ref=dst,
                send_sem=rim_send.at[turn, c, k],
                recv_sem=rim_recv.at[turn, c, k],
                device_id=target,
                device_id_type=MESH,
            )
            for k, (src, dst, target) in enumerate(plan)
        ]

    def tile_of(c, z):
        return pl.ds(pl.multiple_of(c * cell_rows + z * 8, 8), 8)

    def pack(z, value, packed):
        return jnp.where((lane >> 1) == z, pltpu.roll(value, 2 * z + 1, axis=1), packed)

    def send_rims(turn, c, field, packed):
        mine = pl.ds(pl.multiple_of(c * layers, layers), layers)
        x_up, x_down, y_up, y_down = rim_copies(turn, c)
        ys[turn, c] = packed
        start_pair(y_up, y_down, gy, n_gy)
        xs[turn, 0, mine, :] = field[pl.ds(c * cell_rows, layers, stride=8), :]
        xs[turn, 1, mine, :] = field[pl.ds(c * cell_rows + 7, layers, stride=8), :]
        start_pair(x_up, x_down, gx, n_gx)

    def start_pair(up, down, position, count):
        @pl.when(position < count - 1)
        def _():
            up.start()

        @pl.when(position > 0)
        def _():
            down.start()

    def wait_pair(up, down, position, count):
        @pl.when(position < count - 1)
        def _():
            up.wait_send()
            down.wait_recv()

        @pl.when(position > 0)
        def _():
            down.wait_send()
            up.wait_recv()

    def open_rims(turn, c):
        x_up, x_down, y_up, y_down = rim_copies(turn, c)
        wait_pair(x_up, x_down, gx, n_gx)
        wait_pair(y_up, y_down, gy, n_gy)
        return jnp.where((lane & 1) == 0, yr[turn, c, 0], pltpu.roll(yr[turn, c, 1], 126, axis=1))

    def neighbours(turn, field, c, z, columns):
        value = field[tile_of(c, z), :]
        row = c * layers + z
        column = pltpu.roll(columns, 128 - 2 * z, axis=1) if z else columns
        x_low = jnp.broadcast_to(xr[turn, 0, pl.ds(row, 1), :], (8, 128))
        x_high = jnp.broadcast_to(xr[turn, 1, pl.ds(row, 1), :], (8, 128))
        total = jnp.where(sub == 0, x_low, pltpu.roll(value, 1, axis=0))
        total = total + jnp.where(sub == 7, x_high, pltpu.roll(value, 7, axis=0))
        total = total + jnp.where(lane == 0, column, pltpu.roll(value, 1, axis=1))
        total = total + jnp.where(lane == 127, column, pltpu.roll(value, 127, axis=1))
        if z > 0:
            total = total + field[tile_of(c, z - 1), :]
        if z < layers - 1:
            total = total + field[tile_of(c, z + 1), :]
        return value, total

    no_columns = jnp.zeros((8, 128), F32)

    def split_channel(c):
        high, low = halves(state_out[pl.ds(pl.multiple_of(c * cell_rows, cell_rows), cell_rows), :])
        split[c, :, 0:128] = high
        split[c, :, 128:256] = low

    def split_first(c, carry):
        split_channel(c)
        return carry

    lax.fori_loop(0, 4, split_first, 0)

    def block_copy(source, target, source_slot, target_slot, device, send_sem, recv_sem):
        return pltpu.make_async_remote_copy(
            src_ref=source.at[source_slot],
            dst_ref=target.at[target_slot],
            send_sem=send_sem,
            recv_sem=recv_sem,
            device_id=place(device),
            device_id_type=MESH,
        )

    def newton(n, carry):
        turn = n * SWEEPS

        def gather_pair(pair):
            index = jnp.concatenate([cells[pl.ds(2 * pair + k, 1), :] for k in range(2)], axis=1)
            pick = onehot(128, index & 127)
            pick = jnp.concatenate([pick, pick], axis=0)
            wanted = lax.broadcasted_iota(jnp.int32, (cell_rows, 256), 0) == (index >> 7)
            found = []
            for c in range(4):
                value = jnp.dot(split[c], pick, preferred_element_type=F32)
                found.append(jnp.sum(jnp.where(wanted, value, 0.0), axis=0, keepdims=True))
            found = jnp.concatenate(found, axis=0)
            return found[:, :128], found[:, 128:]


        my_pair = lax.div(me, 2)
        pairs = devices // 2

        def pair_of(chunk, k):
            away = 0
            for i, code in enumerate(CHUNK_ORDER):
                away = jnp.where(chunk == i, code, away)
            chip_x = lax.rem(lax.div(gx, 2) + lax.div(away, 4), 4)
            core = lax.rem(gx + 1 - k // 2, 2)
            chip_z = lax.rem(lax.div(gy, 4) + lax.rem(away, 4), 4)
            half_y = lax.rem(lax.div(gy, 2) + 1 - k % 2, 2)
            return (2 * chip_x + core) * (n_gy // 2) + chip_z * 2 + half_y

        def gather_chunk(chunk):
            for k in range(CHUNK):
                pair = pair_of(chunk, k)
                for side, block in enumerate(gather_pair(pair)):
                    send1[n, 2 * pair + side] = block

        def send_block(target):
            block_copy(send1.at[n], recv1.at[n], target, me, target, send1_sem.at[n], recv1_sem.at[n]).start()

        def send_chunk(chunk, count=CHUNK):
            for k in range(count):
                for side in range(2):
                    send_block(2 * pair_of(chunk, k) + side)

        chunks = pairs // CHUNK
        early = chunks // 2

        def early_step(chunk, inner):
            gather_chunk(chunk)
            return inner

        lax.fori_loop(0, early, early_step, 0, unroll=2)

        @pl.when(n == 0)
        def _():
            pl.semaphore_wait(barrier, devices - 1)

            def first_rims(c, rest):
                packed = no_columns
                for z in range(layers):
                    packed = pack(z, state_out[tile_of(c, z), :], packed)
                send_rims(turn, c, state_out, packed)
                return rest

            lax.fori_loop(0, 4, first_rims, 0)

        def late_step(step, inner):
            send_chunk(2 * step)
            gather_chunk(early + step)
            send_chunk(2 * step + 1)
            return inner

        lax.fori_loop(0, chunks - early - 1, late_step, 0)
        send_chunk(chunks - 2)
        gather_chunk(chunks - 1)
        send_chunk(chunks - 1, CHUNK - 1)
        send_block(4 * my_pair + 1 - me)
        recv1[n, me] = send1[n, me]

        @pl.when(n == 0)
        def _():
            for load in loads[2:]:
                load.wait()

            def coefficients(i, inner):
                at = pl.ds(pl.multiple_of(i * 8, 8), 8)
                kinds = rock[at, :]
                picked = [kinds == kind for kind in range(8)]
                for c in range(4):
                    value = jnp.full((8, 128), 6.0, F32)
                    for kind in range(8):
                        value = value + jnp.where(picked[kind], table[c, kind], 0.0)
                    coeff[pl.ds(pl.multiple_of(c * cell_rows + i * 8, 8), 8), :] = value
                return inner

            lax.fori_loop(0, layers, coefficients, 0, unroll=2)
            first = lax.broadcasted_iota(jnp.int32, decay.shape, 0)
            second = lax.broadcasted_iota(jnp.int32, decay.shape, 1)
            gap = (second - first).astype(F32)
            decay[...] = jnp.where(
                gap >= 0, 0.3 * jnp.exp(jnp.maximum(gap, 0.0) * -0.10536051565782628), 0.0
            )

        def base(c, inner):
            columns = open_rims(turn, c)
            for z in range(layers):
                at = tile_of(c, z)
                value, near = neighbours(turn, state_out, c, z, columns)
                square = value * value
                forcing[at, :] = coeff[at, :] * value - near + 0.1 * square * value - right[at, :]
                factor[at, :] = 1.0 / (coeff[at, :] + 0.3 * square)
            return inner

        lax.fori_loop(0, 4, base, 0)

        all_blocks = pl.ds(0, devices - 1)
        arrived = pltpu.make_async_remote_copy(
            src_ref=send1.at[n, all_blocks],
            dst_ref=recv1.at[n, all_blocks],
            send_sem=send1_sem.at[n],
            recv_sem=recv1_sem.at[n],
            device_id=place(me),
            device_id_type=MESH,
        )
        arrived.wait_recv()

        high, low = halves(recv1[n].reshape(4 * devices, 128))
        split2[:, 0:128] = high
        split2[:, 128:256] = low
        quarter = lax.broadcasted_iota(jnp.int32, (4 * devices, 256), 0) >> 2

        def owner_gather(w, inner):
            index = slots[pl.ds(w, 1), :]
            pick = onehot(128, index & 127)
            pick = jnp.concatenate([pick, pick], axis=0)
            value = jnp.dot(split2[...], pick, preferred_element_type=F32)
            value = jnp.where(quarter == (index >> 7), value, 0.0)
            value = jnp.sum(value.reshape(devices // 2, 8, 256), axis=0)
            value = value[0:4] + value[4:8]
            rows[0, pl.ds(w, 4, stride=wells), :] = value[:, :128]
            rows[1, pl.ds(w, 4, stride=wells), :] = value[:, 128:]
            return inner

        lax.fori_loop(0, wells, owner_gather, 0, unroll=16)
        flows = []
        for i in range(4):
            sides = []
            for half in range(2):
                at = slice(half * 128, half * 128 + 128)
                flow = inverse[i, 0, :, at] * rows[half, 0:wells, :]
                for j in range(1, 4):
                    flow = flow + inverse[i, j, :, at] * rows[half, j * wells : (j + 1) * wells, :]
                sides.append(flow)
            flows.append(jnp.concatenate(sides, axis=1))
        rates = jnp.dot(
            jnp.concatenate(flows, axis=0),
            decay[...],
            precision=lax.Precision.HIGHEST,
            preferred_element_type=F32,
        )
        rates_out[...] = rates
        rows[0] = rates[:, :128]
        rows[1] = rates[:, 128:]

        def plane_start(away):
            return lax.rem(my_group + away, PLANES) * group

        def owner_scatter(step):
            first_well = step * WELLS_STEP
            width = WELLS_STEP * 256
            index = jnp.concatenate([slots[pl.ds(first_well + k, 1), :] for k in range(WELLS_STEP)], axis=1)
            rate = jnp.concatenate(
                [rows[half, pl.ds(first_well + k, 4, stride=wells), :] for k in range(WELLS_STEP) for half in range(2)],
                axis=1,
            )
            pick = onehot(256, index & 255)
            wanted = (lax.broadcasted_iota(jnp.int32, (2 * devices, width), 0) >> 2) == (index >> 8)
            parts = []
            for half in halves(jnp.concatenate([rate, rate], axis=0)):
                spread = jnp.broadcast_to(half.astype(F32)[None], (devices // 4, 8, width))
                parts.append(jnp.where(wanted, spread.reshape(2 * devices, width), 0.0).astype(BF16))
            return lax.dot_general(
                jnp.concatenate(parts, axis=1),
                jnp.concatenate([pick, pick], axis=1),
                (((1,), (1,)), ((), ())),
                preferred_element_type=F32,
            )

        def owner_step(step, inner):
            total3[...] += owner_scatter(step)
            return inner

        total3[...] = jnp.zeros_like(total3)
        lax.fori_loop(0, wells // WELLS_STEP, owner_step, 0)
        for k in range(2):
            send2[n, pairs * k : pairs * (k + 1)] = total3[:, 128 * k : 128 * (k + 1)].reshape(pairs, 4, 128)

        def send_slot(device):
            return lax.rem(device, 2) * pairs + lax.div(device, 2)

        def plane_away(j):
            away = 0
            for i, plane in enumerate(PLANE_ORDER):
                away = jnp.where(j == i, plane, away)
            return away

        def return_plane(j, carry):
            start = plane_start(plane_away(j))

            def return_step(step, inner):
                target = start + lax.rem(me + step, group)
                block_copy(
                    send2.at[n], recv2.at[n], send_slot(target), me, target, send2_sem.at[n], recv2_sem.at[n, j]
                ).start()
                return inner

            @pl.when(j > 0)
            def _():
                return_step(0, 0)

            lax.fori_loop(1, group, return_step, 0, unroll=True)
            return carry

        lax.fori_loop(0, PLANES, return_plane, 0)
        recv2[n, me] = send2[n, send_slot(me)]
        arrived.wait_send()


        def wait_group(j, count):
            some = pl.ds(0, count)
            pltpu.make_async_remote_copy(
                src_ref=send2.at[n, some],
                dst_ref=recv2.at[n, some],
                send_sem=send2_sem.at[n],
                recv_sem=recv2_sem.at[n, j],
                device_id=place(me),
                device_id_type=MESH,
            ).wait_recv()

        def owners_of(j):
            return lax.rem(my_group + PLANES - plane_away(j), PLANES) * group

        def cells_of(j, inner):
            start = owners_of(j)
            index = jnp.concatenate([cells[pl.ds(start + k, 1), :] for k in range(group)], axis=1)
            lane_hot[j] = onehot(128, index & 127)
            row_hot[j] = onehot(cell_rows, index >> 7)
            return inner

        @pl.when(n == 0)
        def _():
            lax.fori_loop(0, PLANES, cells_of, 0)

        def inflow_plane(j, inner):
            @pl.when(j == 0)
            def _():
                wait_group(j, group - 1)

            @pl.when(j > 0)
            def _():
                wait_group(j, group)

            start = owners_of(j)
            value = jnp.concatenate([recv2[n, start + k] for k in range(group)], axis=1)
            lanes = lane_hot[j]
            pick = row_hot[j]
            pick = jnp.concatenate([pick, pick], axis=1)
            high, low = halves(value)
            spread = jnp.concatenate(
                [
                    jnp.concatenate([lanes * high[c : c + 1], lanes * low[c : c + 1]], axis=1)
                    for c in range(4)
                ],
                axis=0,
            )
            total4[...] += lax.dot_general(pick, spread, (((1,), (1,)), ((), ())), preferred_element_type=F32)
            return inner

        total4[...] = jnp.zeros_like(total4)
        lax.fori_loop(0, PLANES, inflow_plane, 0)
        sent = pl.ds(0, devices - 1)
        pltpu.make_async_remote_copy(
            src_ref=send2.at[n, sent],
            dst_ref=recv2.at[n, sent],
            send_sem=send2_sem.at[n],
            recv_sem=recv2_sem.at[n, 0],
            device_id=place(me),
            device_id_type=MESH,
        ).wait_send()

        def first_sweep(c, inner):
            packed = no_columns
            for z in range(layers):
                at = tile_of(c, z)
                inflow = total4[z * 8 : z * 8 + 8, pl.ds(pl.multiple_of(c * 128, 128), 128)]
                value = forcing[at, :] - inflow
                forcing[at, :] = value
                value = value * factor[at, :]
                corr[0, at, :] = value
                packed = pack(z, value, packed)
            send_rims(turn + 1, c, corr.at[0], packed)
            return inner

        lax.fori_loop(0, 4, first_sweep, 0)
        for k in range(1, SWEEPS):
            now, later = corr.at[(k - 1) % 2], corr.at[k % 2]

            def sweep(c, inner):
                columns = open_rims(turn + k, c)
                packed = no_columns
                for z in range(layers):
                    at = tile_of(c, z)
                    _, near = neighbours(turn + k, now, c, z, columns)
                    value = (forcing[at, :] + near) * factor[at, :]
                    if k < SWEEPS - 1:
                        later[at, :] = value
                    else:
                        value = state_out[at, :] - value
                        state_out[at, :] = value
                    packed = pack(z, value, packed)
                if k < SWEEPS - 1:
                    send_rims(turn + k + 1, c, later, packed)
                else:

                    @pl.when(n < NEWTON - 1)
                    def _():
                        send_rims(turn + SWEEPS, c, state_out, packed)
                        split_channel(c)

                return inner

            lax.fori_loop(0, 4, sweep, 0)
        return carry

    lax.fori_loop(0, NEWTON, newton, 0)


def on_device(n_gx, n_gy, state_init, right_side, rock_type, trans_table, perf_cells, seg_slot, seg_inverse):
    channels, layers, rows, columns = state_init.shape
    devices = n_gx * n_gy
    wells, segments = seg_slot.shape
    cell_rows = layers * rows
    tiles = channels * layers
    field = (channels * cell_rows, columns)
    vmem = pl.BlockSpec(memory_space=pltpu.VMEM)
    hbm = pl.BlockSpec(memory_space=pl.ANY)
    smem = pl.BlockSpec(memory_space=pltpu.SMEM)
    turns = NEWTON * SWEEPS
    dma = pltpu.SemaphoreType.DMA
    state, rates = pl.pallas_call(
        functools.partial(kernel, n_gx, n_gy, layers, wells),
        out_shape=(
            jax.ShapeDtypeStruct(field, F32),
            jax.ShapeDtypeStruct((channels * wells, segments), F32),
        ),
        in_specs=[hbm, hbm, hbm, smem, hbm, hbm, hbm],
        out_specs=(vmem, vmem),
        scratch_shapes=[
            pltpu.VMEM(field, F32),
            pltpu.VMEM((cell_rows, columns), jnp.int32),
            pltpu.VMEM((devices, perf_cells.shape[2]), jnp.int32),
            pltpu.VMEM((wells, segments), jnp.int32),
            pltpu.VMEM(seg_inverse.shape, F32),
            dma((6,)),
            pltpu.VMEM(field, F32),
            pltpu.VMEM(field, F32),
            pltpu.VMEM(field, F32),
            pltpu.VMEM((2,) + field, F32),
            pltpu.VMEM((channels, cell_rows, 256), BF16),
            pltpu.VMEM((NEWTON, devices, channels, 128), F32),
            pltpu.VMEM((NEWTON, devices, channels, 128), F32),
            pltpu.VMEM((channels * devices, 256), BF16),
            pltpu.VMEM((2, channels * wells, 128), F32),
            pltpu.VMEM((NEWTON, devices, channels, 128), F32),
            pltpu.VMEM((NEWTON, devices, channels, 128), F32),
            pltpu.VMEM((channels * devices // 2, 256), F32),
            pltpu.VMEM((cell_rows, channels * 128), F32),
            pltpu.VMEM((segments, segments), F32),
            pltpu.VMEM((PLANES, 128, devices // PLANES * 128), BF16),
            pltpu.VMEM((PLANES, cell_rows, devices // PLANES * 128), BF16),
            pltpu.VMEM((turns, 2, tiles, 128), F32),
            pltpu.VMEM((turns, 2, tiles, 128), F32),
            pltpu.VMEM((turns, channels, 8, 128), F32),
            pltpu.VMEM((turns, channels, 2, 8, 128), F32),
            dma((NEWTON,)),
            dma((NEWTON,)),
            dma((NEWTON,)),
            dma((NEWTON, PLANES)),
            dma((turns, channels, 4)),
            dma((turns, channels, 4)),
        ],
        compiler_params=pltpu.CompilerParams(
            collective_id=0, has_side_effects=True, vmem_limit_bytes=62 * 1024 * 1024
        ),
        name="newton",
    )(
        state_init.reshape(field),
        right_side.reshape(field),
        rock_type.reshape(cell_rows, columns),
        trans_table,
        perf_cells.reshape(devices, perf_cells.shape[2]),
        seg_slot,
        seg_inverse,
    )
    return state.reshape(state_init.shape), rates.reshape(channels, wells, segments)


def solution(mesh):
    in_specs = (
        P(None, None, "gx", "gy"),
        P(None, None, "gx", "gy"),
        P(None, "gx", "gy"),
        P(),
        P(("gx", "gy"), None, None),
        P(("gx", "gy"), None),
        P(None, None, ("gx", "gy"), None),
    )
    out_specs = (P(None, None, "gx", "gy"), P(None, ("gx", "gy"), None))
    return jax.shard_map(
        functools.partial(on_device, mesh.shape["gx"], mesh.shape["gy"]),
        mesh=mesh,
        in_specs=in_specs,
        out_specs=out_specs,
        check_vma=False,
    )
```
